128 devices in a mesh: rep: 16 (over y, z), grp: 8 (over x, core).
Axes of the slice: x: 4, y: 4, z: 4, core: 2. Of those that a mesh axis runs over, the one named last changes fastest.
Arguments:
- grad_query: float32 [16, 2048, 2048], P('rep', 'grp'), may hold values from -100 to 100, as said below
- error_query: float32 [16, 2048, 2048], P('rep', 'grp'), may hold values from -3 to 3
- basis_query: float32 [2048, 32], replicated, may hold values from -0.125 to 0.125
- momentum_query: float32 [2048, 2048], P('grp'), may hold values from -0.6 to 0.6
- master_query: float32 [2048, 2048], P('grp'), may hold values from -6 to 6
- grad_gate: float32 [16, 2048, 256], P('rep', 'grp'), may hold values from -100 to 100, as said below
- error_gate: float32 [16, 2048, 256], P('rep', 'grp'), may hold values from -3 to 3
- basis_gate: float32 [256, 32], replicated, may hold values from -0.375 to 0.375
- momentum_gate: float32 [2048, 256], P('grp'), may hold values from -0.6 to 0.6
- master_gate: float32 [2048, 256], P('grp'), may hold values from -6 to 6
- vector_grad: float32 [16, 12800], P('rep', 'grp'), may hold values from -6 to 6
- vector_momentum: float32 [12800], P('grp'), may hold values from -0.6 to 0.6
- vector_master: float32 [12800], P('grp'), may hold values from 0.5 to 1.5
Outputs:
- new_error_query: float32 [16, 2048, 2048], P('rep', 'grp')
- new_momentum_query: float32 [2048, 2048], P('grp')
- new_master_query: float32 [2048, 2048], P('grp')
- weight_query: bfloat16 [2048, 2048], replicated
- new_basis_query: float32 [2048, 32], replicated
- new_error_gate: float32 [16, 2048, 256], P('rep', 'grp')
- new_momentum_gate: float32 [2048, 256], P('grp')
- new_master_gate: float32 [2048, 256], P('grp')
- weight_gate: bfloat16 [2048, 256], replicated
- new_basis_gate: float32 [256, 32], replicated
- new_vector_momentum: float32 [12800], P('grp')
- new_vector_master: float32 [12800], P('grp')
- weight_vector: bfloat16 [12800], replicated
The draws below stay inside these ranges and needn't reach their ends.
Inputs may be any that keep to these rules, and one draw needn't show every extreme that they name: `grad_query`: each replica's gradient is a common part plus a replica's own part. `grad_gate`: each replica's gradient is a common part plus a replica's own part.
All inputs are finite; a program needn't handle non-finite values.
Results may differ from the reference program's by a relative error of at most 0.0006.
Values may be sent and summed in bfloat16 or wider, within the bound.
A program may use at most 128 MiB of HBM per device.

```python
import jax
import jax.numpy as jnp
from jax import lax

D = 2048
FQ = 2048
FG = 256
R = 32
VEC = 12800
NS_STEPS = 4
REPLICAS = 16


def gradient_draw(key, columns):
    shared_key = jax.random.fold_in(key, 11)
    own_key = jax.random.fold_in(key, 12)
    rough_key = jax.random.fold_in(key, 13)
    position = jnp.arange(D, dtype=jnp.float32).reshape(1, D, 1) / D
    shared = jnp.clip(jax.random.normal(shared_key, (1, D, columns), jnp.float32), -5.0, 5.0)
    own = jnp.clip(jax.random.normal(own_key, (REPLICAS, D, columns), jnp.float32), -5.0, 5.0)
    rough = jax.random.uniform(rough_key, (1, D, 1), jnp.float32, 0.7, 1.3)
    row_scale = jnp.exp(2.302585 * position) * rough
    return (shared + 0.5 * own) * row_scale


def draw_grad_query(key, part):
    return gradient_draw(key, FQ)


def draw_grad_gate(key, part):
    return gradient_draw(key, FG)


def block_levels(key, extent, shards, least, top_value):
    def one(dim, blocks):
        steps = jax.random.uniform(jax.random.fold_in(jax.random.fold_in(key, 6), dim), (blocks,), jnp.float32, least / len(shards), top_value / len(shards))
        return jnp.repeat(jnp.exp(steps), extent[dim] // blocks).reshape((-1,) + (1,) * (len(extent) - dim - 1))

    gain = one(*shards[0])
    for cut in shards[1:]:
        gain = gain * one(*cut)
    return gain


def noise(key, shape, deviation, reach, shards=(), kind=jnp.bfloat16):
    values = jax.random.normal(key, shape, jnp.float32) * deviation
    if len(shards) > 0:
        values = block_levels(key, shape, shards, -0.22, 0.18) * values
    return jnp.clip(values, min=-reach, max=reach).astype(kind)


def setup_inputs(seed: int = 0) -> dict:
    seeds = jax.random.split(jax.random.key(seed), 14)
    grad_query = draw_grad_query(jax.random.fold_in(seeds[13], 71), 0)
    error_query = noise(seeds[1], (REPLICAS, D, FQ), 0.5, 3.0, ((0, 16), (1, 8)), jnp.float32)
    basis_query = noise(seeds[2], (FQ, R), FQ ** -0.5, 0.125, (), jnp.float32)
    momentum_query = noise(seeds[3], (D, FQ), 0.1, 0.6, ((0, 8),), jnp.float32)
    master_query = noise(seeds[4], (D, FQ), 1.0, 6.0, ((0, 8),), jnp.float32)
    grad_gate = draw_grad_gate(jax.random.fold_in(seeds[13], 71), 0)
    error_gate = noise(seeds[6], (REPLICAS, D, FG), 0.5, 3.0, ((0, 16), (1, 8)), jnp.float32)
    basis_gate = noise(seeds[7], (FG, R), FG ** -0.5, 0.375, (), jnp.float32)
    momentum_gate = noise(seeds[8], (D, FG), 0.1, 0.6, ((0, 8),), jnp.float32)
    master_gate = noise(seeds[9], (D, FG), 1.0, 6.0, ((0, 8),), jnp.float32)
    vector_grad = noise(seeds[10], (REPLICAS, VEC), 1.0, 6.0, ((0, 16), (1, 8)), jnp.float32)
    vector_momentum = noise(seeds[11], (VEC,), 0.1, 0.6, ((0, 8),), jnp.float32)
    vector_master = jnp.clip(1.0 + 0.1 * jax.random.normal(seeds[12], (VEC,), jnp.float32), 0.5, 1.5)
    return {"grad_query": grad_query, "error_query": error_query, "basis_query": basis_query, "momentum_query": momentum_query, "master_query": master_query, "grad_gate": grad_gate, "error_gate": error_gate, "basis_gate": basis_gate, "momentum_gate": momentum_gate, "master_gate": master_gate, "vector_grad": vector_grad, "vector_momentum": vector_momentum, "vector_master": vector_master}


highest = lax.Precision.HIGHEST

def inverse_root(gram_matrix):
    trace_value = jnp.trace(gram_matrix)
    identity = jnp.eye(gram_matrix.shape[0], dtype=jnp.float32)
    root_part = gram_matrix / trace_value
    inverse_part = identity
    for iteration in range(NS_STEPS):
        middle = 0.5 * (3.0 * identity - jnp.dot(inverse_part, root_part, precision=highest))
        root_part = jnp.dot(root_part, middle, precision=highest)
        inverse_part = jnp.dot(middle, inverse_part, precision=highest)
    return inverse_part / jnp.sqrt(trace_value)

def compress(grad, error, basis, momentum, master):
    merged = grad + error
    left_factor = jnp.einsum('kdn,nr->dr', merged, basis, precision=highest)
    gram_matrix = jnp.dot(left_factor.T, left_factor, precision=highest)
    ortho = jnp.dot(left_factor, inverse_root(gram_matrix), precision=highest)
    new_basis = jnp.einsum('kdn,dr->nr', merged, ortho, precision=highest)
    approx = jnp.dot(ortho, new_basis.T, precision=highest) / REPLICAS
    new_error = merged - approx[None]
    new_momentum = 0.9 * momentum + approx
    new_master = master - 0.5 * new_momentum
    return (new_error, new_momentum, new_master, new_master.astype(jnp.bfloat16), new_basis)

def reference(grad_query, error_query, basis_query, momentum_query, master_query, grad_gate, error_gate, basis_gate, momentum_gate, master_gate, vector_grad, vector_momentum, vector_master):
    out_query = compress(grad_query, error_query, basis_query, momentum_query, master_query)
    out_gate = compress(grad_gate, error_gate, basis_gate, momentum_gate, master_gate)
    vector_mean = lax.optimization_barrier(jnp.sum(vector_grad, axis=0)) / REPLICAS
    new_vector_momentum = 0.9 * vector_momentum + vector_mean
    new_vector_master = vector_master - 0.5 * new_vector_momentum
    return (out_query[0], out_query[1], out_query[2], out_query[3], out_query[4], out_gate[0], out_gate[1], out_gate[2], out_gate[3], out_gate[4], new_vector_momentum, new_vector_master, new_vector_master.astype(jnp.bfloat16))
```

```python
import functools

import jax
import jax.numpy as jnp
from jax import lax
from jax.experimental import pallas as pl
from jax.experimental.pallas import tpu as pltpu
from jax.sharding import PartitionSpec as P

NS_STEPS = 4
RANK = 32
BOTH = 2 * RANK
HIGHEST = lax.Precision.HIGHEST
F32 = jnp.float32
BF16 = jnp.bfloat16
VMEM = pltpu.VMEM
NT = (((1,), (1,)), ((), ()))


def split(x):
    high = x.astype(BF16)
    return high, (x - high.astype(F32)).astype(BF16)


def mm(a, b, dims=(((1,), (0,)), ((), ()))):
    return lax.dot_general(a, b, dims, preferred_element_type=F32)


def three_pass(a_high, a_low, b_high, b_low, dims=(((1,), (0,)), ((), ()))):
    rows = a_high.shape[0]
    both = mm(jnp.concatenate([a_high, a_low], axis=0), b_high, dims)
    return both[:rows] + both[rows:] + mm(a_high, b_low, dims)


def full_dot(a, b):
    return jnp.dot(a, b, precision=HIGHEST, preferred_element_type=F32)


def inverse_roots(query_gram, gate_gram):
    row = lax.broadcasted_iota(jnp.int32, (BOTH, BOTH), 0)
    column = lax.broadcasted_iota(jnp.int32, (BOTH, BOTH), 1)
    identity = (row == column).astype(F32)
    zero = jnp.zeros((RANK, RANK), F32)
    gram = jnp.concatenate(
        [
            jnp.concatenate([query_gram, zero], axis=1),
            jnp.concatenate([zero, gate_gram], axis=1),
        ],
        axis=0,
    )
    diagonal = jnp.sum(gram * identity, axis=1, keepdims=True)
    is_query = lax.broadcasted_iota(jnp.int32, (BOTH, 1), 0) < RANK
    query_trace = jnp.sum(jnp.where(is_query, diagonal, 0.0), axis=0, keepdims=True)
    gate_trace = jnp.sum(jnp.where(is_query, 0.0, diagonal), axis=0, keepdims=True)
    trace = jnp.where(is_query, query_trace, gate_trace)
    root = gram / trace
    middle = 0.5 * (3.0 * identity - root)
    inverse = middle
    for step in range(1, NS_STEPS):
        root = full_dot(root, middle)
        middle = 0.5 * (3.0 * identity - full_dot(inverse, root))
        inverse = full_dot(middle, inverse)
    return inverse / jnp.sqrt(trace)


def factor_kernel(
    reps,
    grps,
    grad_query,
    error_query,
    basis_query,
    grad_gate,
    error_gate,
    basis_gate,
    vector_grad,
    vector_momentum,
    vector_master,
    ortho_out,
    right_out,
    momentum_out,
    master_out,
    weight_out,
    grad_in,
    error_in,
    merged_high,
    merged_low,
    left_send,
    left_recv,
    left_sum,
    left_all,
    left,
    gram_all,
    vector_rows,
    vector_send,
    vector_all,
    vector_place,
    right_send,
    right_recv,
    right_part,
    right_final,
    right_all,
    load_sem,
    rep_send,
    rep_recv,
    grp_send,
    grp_recv,
):
    me = lax.axis_index("rep")
    my = lax.axis_index("grp")
    columns = grad_query.shape[1]
    gate = grad_gate.shape[1]
    step = 512
    pieces = [(i * step, step, i) for i in range(columns // step)]
    pieces.append((columns, gate, len(pieces)))

    def loads(start, size, index):
        if start < columns:
            grad, error, place = grad_query, error_query, pl.ds(start, size)
        else:
            grad, error, place = grad_gate, error_gate, pl.ds(0, size)
        into = pl.ds(start, size)
        return (
            pltpu.make_async_copy(
                grad.at[:, place], grad_in.at[:, into], load_sem.at[0, index]
            ),
            pltpu.make_async_copy(
                error.at[:, place], error_in.at[:, into], load_sem.at[1, index]
            ),
        )

    for piece in pieces:
        for copy in loads(*piece):
            copy.start()

    barrier = pltpu.get_barrier_semaphore()

    def greet_rep(d, carry):
        pl.semaphore_signal(barrier, inc=1, device_id={"rep": lax.rem(me + d, reps)})
        return carry

    def greet_grp(d, carry):
        pl.semaphore_signal(barrier, inc=1, device_id={"grp": lax.rem(my + d, grps)})
        return carry

    lax.fori_loop(1, reps, greet_rep, 0)
    lax.fori_loop(1, grps, greet_grp, 0)

    def to_peers(phase, axis, source, target):
        size, index = (reps, me) if axis == "rep" else (grps, my)
        send, recv = (rep_send, rep_recv) if axis == "rep" else (grp_send, grp_recv)

        def copy(d, at):
            peer = lax.rem(index + d, size)
            return pltpu.make_async_remote_copy(
                src_ref=source(peer),
                dst_ref=target.at[at],
                send_sem=send.at[phase, d],
                recv_sem=recv.at[phase, at],
                device_id={axis: peer},
            )

        def start(d, carry):
            copy(d, index).start()
            return carry

        def await_recv(d, carry):
            copy(d, lax.rem(index + d, size)).wait_recv()
            return carry

        def await_send(d, carry):
            copy(d, index).wait_send()
            return carry

        return (
            lambda: lax.fori_loop(1, size, start, 0),
            lambda: lax.fori_loop(1, size, await_recv, 0),
            lambda: lax.fori_loop(1, size, await_send, 0),
        )

    left_query = jnp.zeros((RANK, grad_query.shape[0]), F32)
    left_gate = left_query
    for start, size, index in pieces:
        for copy in loads(start, size, index):
            copy.wait()
        at = slice(start, start + size)
        high, low = split(grad_in[:, at] + error_in[:, at])
        merged_high[:, at] = high
        merged_low[:, at] = low
        if start < columns:
            basis = split(basis_query[:, at])
            left_query += three_pass(*basis, high, low, NT)
        else:
            basis = split(basis_gate[...])
            left_gate += three_pass(*basis, high, low, NT)

    length = vector_grad.shape[1]
    lines = -(-length // 128)
    own = jnp.concatenate([left_query, left_gate], axis=0)
    share = BOTH // reps
    left_send[...] = jnp.zeros_like(left_send)
    for i in range(reps):
        left_send[i, 0:share, :] = own[i * share : (i + 1) * share]
    for i in range(lines):
        width = min(128, length - i * 128)
        left_send[i, share : share + 1, 0:width] = vector_grad[:, i * 128 : i * 128 + width]

    pl.semaphore_wait(barrier, reps - 1 + grps - 1)

    start_1, recv_1, send_1 = to_peers(0, "rep", lambda peer: left_send.at[peer], left_recv)
    start_1()
    left_recv[me] = left_send[me]
    recv_1()
    total = left_recv[0]
    for i in range(1, reps):
        total += left_recv[i]
    left_sum[...] = total

    start_2, recv_2, send_2 = to_peers(1, "rep", lambda peer: left_sum, left_all)
    start_2()
    left_all[me] = total
    recv_2()
    for i in range(reps):
        left[i * share : (i + 1) * share, :] = left_all[i, 0:share, :]

    left_high, left_low = split(left[...])
    grams = []
    for part in (slice(0, RANK), slice(RANK, BOTH)):
        grams.append(
            three_pass(left_high[part], left_low[part], left_high[part], left_low[part], NT)
        )
    half = RANK // 2
    gram_all[my] = jnp.concatenate(
        [grams[0][:half], grams[0][half:], grams[1][:half], grams[1][half:]], axis=1
    )
    start_3, recv_3, send_3 = to_peers(0, "grp", lambda peer: gram_all.at[my], gram_all)
    start_3()

    vector_rows[...] = jnp.zeros_like(vector_rows)
    for i in range(lines):
        width = min(128, length - i * 128)
        at = slice(i * 128, i * 128 + width)
        mean = left_all[i, share : share + 1, 0:width] / reps
        new_momentum = 0.9 * vector_momentum[:, at] + mean
        new_master = vector_master[:, at] - 0.5 * new_momentum
        momentum_out[:, at] = new_momentum
        master_out[:, at] = new_master
        vector_rows[i : i + 1, 0:width] = new_master
    vector_send[...] = vector_rows[...].astype(BF16)
    start_v, recv_v, send_v = to_peers(1, "grp", lambda peer: vector_send, vector_all)
    start_v()
    vector_all[my] = vector_send[...]

    recv_3()
    gram = gram_all[0]
    for i in range(1, grps):
        gram += gram_all[i]
    quarters = [gram[:, i * RANK : (i + 1) * RANK] for i in range(4)]
    query_gram = jnp.concatenate(
        [quarters[0][:, 0:RANK], quarters[1][:, 0:RANK]], axis=0
    )
    gate_gram = jnp.concatenate([quarters[2], quarters[3]], axis=0)
    inverse = inverse_roots(query_gram, gate_gram)
    ortho = full_dot(inverse, left[...])
    ortho_out[...] = ortho
    ortho_high, ortho_low = split(ortho)

    rows = RANK // reps
    for start, size, index in pieces:
        at = slice(start, start + size)
        part = slice(0, RANK) if start < columns else slice(RANK, BOTH)
        terms = three_pass(
            ortho_high[part], ortho_low[part], merged_high[:, at], merged_low[:, at]
        )
        for i in range(reps):
            right_send[i, :, at] = terms[i * rows : (i + 1) * rows]
    start_4, recv_4, send_4 = to_peers(2, "rep", lambda peer: right_send.at[peer], right_recv)
    start_4()
    right_recv[me] = right_send[me]
    recv_4()
    total = right_recv[0]
    for i in range(1, reps):
        total += right_recv[i]

    right_part[my] = total
    start_5, recv_5, send_5 = to_peers(2, "grp", lambda peer: right_part.at[my], right_part)
    start_5()
    recv_5()
    total = right_part[0]
    for i in range(1, grps):
        total += right_part[i]
    right_final[...] = total

    start_6, recv_6, send_6 = to_peers(3, "rep", lambda peer: right_final, right_all)
    start_6()
    right_all[me] = total

    recv_v()
    low_lanes = lax.broadcasted_iota(jnp.int32, (lines - 1, 128), 1) < 64
    low_lane = lax.broadcasted_iota(jnp.int32, (1, 128), 1) < 64
    for i in range(grps // 2):
        base = i * 2 * length // 128
        even = vector_all[2 * i].astype(F32)
        odd = pltpu.roll(vector_all[2 * i + 1].astype(F32), 64, 1)
        vector_place[base : base + lines - 1, :] = even[: lines - 1]
        vector_place[base + lines - 1 : base + lines, :] = jnp.where(
            low_lane, even[lines - 1 : lines], odd[0:1]
        )
        vector_place[base + lines : base + 2 * lines - 1, :] = jnp.where(
            low_lanes, odd[: lines - 1], odd[1:lines]
        )
    weight_out[...] = vector_place[0 : weight_out.shape[0], :].astype(BF16)

    recv_6()
    for i in range(reps):
        right_out[i * rows : (i + 1) * rows, :] = right_all[i]
    for wait in (send_1, send_2, send_3, send_v, send_4, send_5, send_6):
        wait()


def finish_kernel(
    reps,
    ortho,
    right_query,
    right_gate,
    grad_query,
    error_query,
    momentum_query,
    master_query,
    grad_gate,
    error_gate,
    momentum_gate,
    master_gate,
    error_out_query,
    momentum_out_query,
    master_out_query,
    weight_out_query,
    error_out_gate,
    momentum_out_gate,
    master_out_gate,
    weight_out_gate,
    left_parts,
):
    @pl.when(pl.program_id(0) == 0)
    def _():
        for part, at in ((slice(0, RANK), 0), (slice(RANK, BOTH), 1)):
            high, low = split(ortho[part, :].T / reps)
            left_parts[at] = jnp.concatenate([high, high, low], axis=1)

    def update(index, right, grad, error, momentum, master, outs):
        high, low = split(right[...])
        approx = mm(left_parts[index], jnp.concatenate([high, low, high], axis=0))
        outs[0][...] = (grad[...] + error[...]) - approx
        new_momentum = 0.9 * momentum[...] + approx
        outs[1][...] = new_momentum
        new_master = master[...] - 0.5 * new_momentum
        outs[2][...] = new_master
        outs[3][...] = new_master.astype(BF16)

    update(
        0,
        right_query,
        grad_query,
        error_query,
        momentum_query,
        master_query,
        (error_out_query, momentum_out_query, master_out_query, weight_out_query),
    )

    @pl.when(pl.program_id(0) == 0)
    def _():
        update(
            1,
            right_gate,
            grad_gate,
            error_gate,
            momentum_gate,
            master_gate,
            (error_out_gate, momentum_out_gate, master_out_gate, weight_out_gate),
        )


def per_device(
    grad_query,
    error_query,
    basis_query,
    momentum_query,
    master_query,
    grad_gate,
    error_gate,
    basis_gate,
    momentum_gate,
    master_gate,
    vector_grad,
    vector_momentum,
    vector_master,
):
    reps, grps = lax.axis_size("rep"), lax.axis_size("grp")
    grad_query, error_query = grad_query[0], error_query[0]
    grad_gate, error_gate = grad_gate[0], error_gate[0]
    rows, columns = grad_query.shape
    gate = grad_gate.shape[1]
    both = columns + gate
    length = vector_grad.shape[1]
    share = RANK // reps
    any_spec = pl.BlockSpec(memory_space=pl.ANY)
    vmem_spec = pl.BlockSpec(memory_space=VMEM)
    ortho, right, vec_momentum, vec_master, vec_weight = pl.pallas_call(
        functools.partial(factor_kernel, reps, grps),
        out_shape=(
            jax.ShapeDtypeStruct((BOTH, rows), F32),
            jax.ShapeDtypeStruct((RANK, both), F32),
            jax.ShapeDtypeStruct((1, length), F32),
            jax.ShapeDtypeStruct((1, length), F32),
            jax.ShapeDtypeStruct((grps * length // 128, 128), BF16),
        ),
        in_specs=[
            any_spec,
            any_spec,
            vmem_spec,
            any_spec,
            any_spec,
            vmem_spec,
            vmem_spec,
            vmem_spec,
            vmem_spec,
        ],
        out_specs=[vmem_spec] * 5,
        scratch_shapes=[
            VMEM((rows, both), F32),
            VMEM((rows, both), F32),
            VMEM((rows, both), BF16),
            VMEM((rows, both), BF16),
            VMEM((reps, 8, rows), F32),
            VMEM((reps, 8, rows), F32),
            VMEM((8, rows), F32),
            VMEM((reps, 8, rows), F32),
            VMEM((BOTH, rows), F32),
            VMEM((grps, RANK // 2, 4 * RANK), F32),
            VMEM((16, 128), F32),
            VMEM((16, 128), BF16),
            VMEM((grps, 16, 128), BF16),
            VMEM((104, 128), F32),
            VMEM((reps, share, both), F32),
            VMEM((reps, share, both), F32),
            VMEM((grps, share, both), F32),
            VMEM((share, both), F32),
            VMEM((reps, share, both), F32),
            pltpu.SemaphoreType.DMA((2, columns // 512 + 1)),
            pltpu.SemaphoreType.DMA((4, reps)),
            pltpu.SemaphoreType.DMA((4, reps)),
            pltpu.SemaphoreType.DMA((3, grps)),
            pltpu.SemaphoreType.DMA((3, grps)),
        ],
        compiler_params=pltpu.CompilerParams(collective_id=0, has_side_effects=True),
        name="factors",
    )(
        grad_query,
        error_query,
        basis_query.T,
        grad_gate,
        error_gate,
        basis_gate.T,
        vector_grad,
        vector_momentum.reshape(1, length),
        vector_master.reshape(1, length),
    )

    tile = 256
    query_spec = pl.BlockSpec((rows, tile), lambda i: (0, i))
    gate_spec = pl.BlockSpec((rows, gate), lambda i: (0, 0))
    f32_query = jax.ShapeDtypeStruct((rows, columns), F32)
    f32_gate = jax.ShapeDtypeStruct((rows, gate), F32)
    outs = pl.pallas_call(
        functools.partial(finish_kernel, reps),
        grid=(columns // tile,),
        out_shape=(f32_query,) * 3
        + (jax.ShapeDtypeStruct((rows, columns), BF16),)
        + (f32_gate,) * 3
        + (jax.ShapeDtypeStruct((rows, gate), BF16),),
        in_specs=[
            pl.BlockSpec((BOTH, rows), lambda i: (0, 0)),
            pl.BlockSpec((RANK, tile), lambda i: (0, i)),
            pl.BlockSpec((RANK, gate), lambda i: (0, columns // gate)),
        ]
        + [query_spec] * 4
        + [gate_spec] * 4,
        out_specs=[query_spec] * 4 + [gate_spec] * 4,
        scratch_shapes=[VMEM((2, rows, 3 * RANK), BF16)],
        name="finish",
    )(
        ortho,
        right,
        right,
        grad_query,
        error_query,
        momentum_query,
        master_query,
        grad_gate,
        error_gate,
        momentum_gate,
        master_gate,
    )
    whole_query = lax.all_gather(outs[3], "grp", axis=0, tiled=True)
    whole_gate = lax.all_gather(outs[7], "grp", axis=0, tiled=True)
    return (
        outs[0][None],
        outs[1],
        outs[2],
        whole_query,
        right[:, :columns].T,
        outs[4][None],
        outs[5],
        outs[6],
        whole_gate,
        right[:, columns:].T,
        vec_momentum.reshape(length),
        vec_master.reshape(length),
        vec_weight.reshape(grps * length),
    )


def solution(mesh):
    in_specs = (
        P("rep", "grp", None),
        P("rep", "grp", None),
        P(),
        P("grp", None),
        P("grp", None),
        P("rep", "grp", None),
        P("rep", "grp", None),
        P(),
        P("grp", None),
        P("grp", None),
        P("rep", "grp"),
        P("grp"),
        P("grp"),
    )
    out_specs = (
        P("rep", "grp", None),
        P("grp", None),
        P("grp", None),
        P(),
        P(),
        P("rep", "grp", None),
        P("grp", None),
        P("grp", None),
        P(),
        P(),
        P("grp"),
        P("grp"),
        P(),
    )
    return jax.shard_map(
        per_device, mesh=mesh, in_specs=in_specs, out_specs=out_specs, check_vma=False
    )
```

```python
import functools

import jax
import jax.numpy as jnp
from jax import lax
from jax.experimental import pallas as pl
from jax.experimental.pallas import tpu as pltpu
from jax.sharding import PartitionSpec as P

NS_STEPS = 4
RANK = 32
BOTH = 2 * RANK
HIGHEST = lax.Precision.HIGHEST
F32 = jnp.float32
BF16 = jnp.bfloat16
VMEM = pltpu.VMEM
NT = (((1,), (1,)), ((), ()))


def split(x):
    high = x.astype(BF16)
    return high, (x - high.astype(F32)).astype(BF16)


def mm(a, b, dims=(((1,), (0,)), ((), ()))):
    return lax.dot_general(a, b, dims, preferred_element_type=F32)


def three_pass(a_high, a_low, b_high, b_low, dims=(((1,), (0,)), ((), ()))):
    rows = a_high.shape[0]
    both = mm(jnp.concatenate([a_high, a_low], axis=0), b_high, dims)
    return both[:rows] + both[rows:] + mm(a_high, b_low, dims)


def full_dot(a, b):
    return jnp.dot(a, b, precision=HIGHEST, preferred_element_type=F32)


def inverse_roots(query_gram, gate_gram):
    row = lax.broadcasted_iota(jnp.int32, (BOTH, BOTH), 0)
    column = lax.broadcasted_iota(jnp.int32, (BOTH, BOTH), 1)
    identity = (row == column).astype(F32)
    zero = jnp.zeros((RANK, RANK), F32)
    gram = jnp.concatenate(
        [
            jnp.concatenate([query_gram, zero], axis=1),
            jnp.concatenate([zero, gate_gram], axis=1),
        ],
        axis=0,
    )
    diagonal = jnp.sum(gram * identity, axis=1, keepdims=True)
    is_query = lax.broadcasted_iota(jnp.int32, (BOTH, 1), 0) < RANK
    query_trace = jnp.sum(jnp.where(is_query, diagonal, 0.0), axis=0, keepdims=True)
    gate_trace = jnp.sum(jnp.where(is_query, 0.0, diagonal), axis=0, keepdims=True)
    trace = jnp.where(is_query, query_trace, gate_trace)
    root = gram / trace
    middle = 0.5 * (3.0 * identity - root)
    inverse = middle
    for step in range(1, NS_STEPS):
        root = full_dot(root, middle)
        middle = 0.5 * (3.0 * identity - full_dot(inverse, root))
        inverse = full_dot(middle, inverse)
    return inverse / jnp.sqrt(trace)


def factor_kernel(
    reps,
    grps,
    grad_query,
    error_query,
    basis_query,
    grad_gate,
    error_gate,
    basis_gate,
    vector_grad,
    vector_momentum,
    vector_master,
    momentum_query,
    master_query,
    momentum_gate,
    master_gate,
    right_out,
    momentum_out,
    master_out,
    weight_out,
    new_error,
    new_momentum,
    new_master,
    weights,
    grad_in,
    error_in,
    momentum_in,
    master_in,
    merged_high,
    merged_low,
    left_send,
    left_recv,
    left_sum,
    left_all,
    left,
    gram_all,
    vector_rows,
    vector_send,
    vector_all,
    vector_place,
    right_send,
    right_recv,
    right_part,
    right_final,
    right_all,
    load_sem,
    rep_send,
    rep_recv,
    grp_send,
    grp_recv,
    x_send,
    x_recv,
    plane_send,
    plane_recv,
    core_send,
    core_recv,
):
    me = lax.axis_index("rep")
    my = lax.axis_index("grp")
    columns = grad_query.shape[1]
    gate = grad_gate.shape[1]
    step = 512
    pieces = [(i * step, step, i) for i in range(columns // step)]
    pieces.append((columns, gate, len(pieces)))

    def loads(start, size, index):
        if start < columns:
            grad, error, place = grad_query, error_query, pl.ds(start, size)
        else:
            grad, error, place = grad_gate, error_gate, pl.ds(0, size)
        into = pl.ds(start, size)
        return (
            pltpu.make_async_copy(
                grad.at[:, place], grad_in.at[:, into], load_sem.at[0, index]
            ),
            pltpu.make_async_copy(
                error.at[:, place], error_in.at[:, into], load_sem.at[1, index]
            ),
        )

    for piece in pieces:
        for copy in loads(*piece):
            copy.start()

    later = [
        pltpu.make_async_copy(source, into.at[:, at], load_sem.at[2 + i, j])
        for i, (into, pair) in enumerate(
            (
                (momentum_in, (momentum_query, momentum_gate)),
                (master_in, (master_query, master_gate)),
            )
        )
        for j, (source, at) in enumerate(zip(pair, (pl.ds(0, columns), pl.ds(columns, gate))))
    ]
    for copy in later:
        copy.start()

    barrier = pltpu.get_barrier_semaphore()

    def greet_rep(d, carry):
        pl.semaphore_signal(barrier, inc=1, device_id={"rep": lax.rem(me + d, reps)})
        return carry

    def greet_grp(d, carry):
        pl.semaphore_signal(barrier, inc=1, device_id={"grp": lax.rem(my + d, grps)})
        return carry

    lax.fori_loop(1, reps, greet_rep, 0)
    lax.fori_loop(1, grps, greet_grp, 0)

    def to_peers(phase, axis, source, target):
        size, index = (reps, me) if axis == "rep" else (grps, my)
        send, recv = (rep_send, rep_recv) if axis == "rep" else (grp_send, grp_recv)

        def copy(d, at):
            peer = lax.rem(index + d, size)
            return pltpu.make_async_remote_copy(
                src_ref=source(peer),
                dst_ref=target.at[at],
                send_sem=send.at[phase, d],
                recv_sem=recv.at[phase, at],
                device_id={axis: peer},
            )

        def start(d, carry):
            copy(d, index).start()
            return carry

        def await_recv(d, carry):
            copy(d, lax.rem(index + d, size)).wait_recv()
            return carry

        def await_send(d, carry):
            copy(d, index).wait_send()
            return carry

        return (
            lambda: lax.fori_loop(1, size, start, 0),
            lambda: lax.fori_loop(1, size, await_recv, 0),
            lambda: lax.fori_loop(1, size, await_send, 0),
        )

    left_query = jnp.zeros((RANK, grad_query.shape[0]), F32)
    left_gate = left_query
    for start, size, index in pieces:
        for copy in loads(start, size, index):
            copy.wait()
        at = slice(start, start + size)
        high, low = split(grad_in[:, at] + error_in[:, at])
        merged_high[:, at] = high
        merged_low[:, at] = low
        if start < columns:
            basis = split(basis_query[:, at])
            left_query += three_pass(*basis, high, low, NT)
        else:
            basis = split(basis_gate[...])
            left_gate += three_pass(*basis, high, low, NT)

    length = vector_grad.shape[1]
    lines = -(-length // 128)
    own = jnp.concatenate([left_query, left_gate], axis=0)
    share = BOTH // reps
    left_send[...] = jnp.zeros_like(left_send)
    for i in range(reps):
        left_send[i, 0:share, :] = own[i * share : (i + 1) * share]
    for i in range(lines):
        width = min(128, length - i * 128)
        left_send[i, share : share + 1, 0:width] = vector_grad[:, i * 128 : i * 128 + width]

    pl.semaphore_wait(barrier, reps - 1 + grps - 1)

    start_1, recv_1, send_1 = to_peers(0, "rep", lambda peer: left_send.at[peer], left_recv)
    start_1()
    left_recv[me] = left_send[me]
    recv_1()
    total = left_recv[0]
    for i in range(1, reps):
        total += left_recv[i]
    left_sum[...] = total

    start_2, recv_2, send_2 = to_peers(1, "rep", lambda peer: left_sum, left_all)
    start_2()
    left_all[me] = total
    recv_2()
    for i in range(reps):
        left[i * share : (i + 1) * share, :] = left_all[i, 0:share, :]

    left_high, left_low = split(left[...])
    grams = []
    for part in (slice(0, RANK), slice(RANK, BOTH)):
        grams.append(
            three_pass(left_high[part], left_low[part], left_high[part], left_low[part], NT)
        )
    half = RANK // 2
    gram_all[my] = jnp.concatenate(
        [grams[0][:half], grams[0][half:], grams[1][:half], grams[1][half:]], axis=1
    )
    start_3, recv_3, send_3 = to_peers(0, "grp", lambda peer: gram_all.at[my], gram_all)
    start_3()

    vector_rows[...] = jnp.zeros_like(vector_rows)
    for i in range(lines):
        width = min(128, length - i * 128)
        at = slice(i * 128, i * 128 + width)
        mean = left_all[i, share : share + 1, 0:width] / reps
        gain_momentum = 0.9 * vector_momentum[:, at] + mean
        gain = vector_master[:, at] - 0.5 * gain_momentum
        momentum_out[:, at] = gain_momentum
        master_out[:, at] = gain
        vector_rows[i : i + 1, 0:width] = gain
    vector_send[...] = vector_rows[...].astype(BF16)
    start_v, recv_v, send_v = to_peers(1, "grp", lambda peer: vector_send, vector_all)
    start_v()
    vector_all[my] = vector_send[...]

    recv_3()
    gram = gram_all[0]
    for i in range(1, grps):
        gram += gram_all[i]
    quarters = [gram[:, i * RANK : (i + 1) * RANK] for i in range(4)]
    query_gram = jnp.concatenate(
        [quarters[0][:, 0:RANK], quarters[1][:, 0:RANK]], axis=0
    )
    gate_gram = jnp.concatenate([quarters[2], quarters[3]], axis=0)
    inverse = inverse_roots(query_gram, gate_gram)
    ortho = full_dot(inverse, left[...])
    ortho_high, ortho_low = split(ortho)

    rows = RANK // reps
    for start, size, index in pieces:
        at = slice(start, start + size)
        part = slice(0, RANK) if start < columns else slice(RANK, BOTH)
        terms = three_pass(
            ortho_high[part], ortho_low[part], merged_high[:, at], merged_low[:, at]
        )
        for i in range(reps):
            right_send[i, :, at] = terms[i * rows : (i + 1) * rows]
    start_4, recv_4, send_4 = to_peers(2, "rep", lambda peer: right_send.at[peer], right_recv)
    start_4()
    right_recv[me] = right_send[me]
    recv_4()
    total = right_recv[0]
    for i in range(1, reps):
        total += right_recv[i]

    right_part[my] = total
    start_5, recv_5, send_5 = to_peers(2, "grp", lambda peer: right_part.at[my], right_part)
    start_5()
    recv_5()
    total = right_part[0]
    for i in range(1, grps):
        total += right_part[i]
    right_final[...] = total

    start_6, recv_6, send_6 = to_peers(3, "rep", lambda peer: right_final, right_all)
    start_6()
    right_all[me] = total

    recv_v()
    low_lanes = lax.broadcasted_iota(jnp.int32, (lines - 1, 128), 1) < 64
    low_lane = lax.broadcasted_iota(jnp.int32, (1, 128), 1) < 64
    for i in range(grps // 2):
        base = i * 2 * length // 128
        even = vector_all[2 * i].astype(F32)
        odd = pltpu.roll(vector_all[2 * i + 1].astype(F32), 64, 1)
        vector_place[base : base + lines - 1, :] = even[: lines - 1]
        vector_place[base + lines - 1 : base + lines, :] = jnp.where(
            low_lane, even[lines - 1 : lines], odd[0:1]
        )
        vector_place[base + lines : base + 2 * lines - 1, :] = jnp.where(
            low_lanes, odd[: lines - 1], odd[1:lines]
        )
    weight_out[...] = vector_place[0 : weight_out.shape[0], :].astype(BF16)

    recv_6()
    for i in range(reps):
        right_out[i * rows : (i + 1) * rows, :] = right_all[i]

    for copy in later:
        copy.wait()
    block = grad_query.shape[0]
    factors = []
    for part in (slice(0, RANK), slice(RANK, BOTH)):
        high, low = split(ortho[part].T / reps)
        factors.append(jnp.concatenate([high, high, low], axis=1))
    own_rows = pl.ds(pl.multiple_of(my * block, block), block)
    tiles = [(start, 256) for start in range(0, columns + gate, 256)]
    for start, size in tiles:
        at = slice(start, start + size)
        high, low = split(right_out[:, at])
        approx = mm(
            factors[0 if start < columns else 1],
            jnp.concatenate([high, low, high], axis=0),
        )
        new_error[:, at] = approx
        moved = 0.9 * momentum_in[:, at] + approx
        new_momentum[:, at] = moved
        updated = master_in[:, at] - 0.5 * moved
        new_master[:, at] = updated
        weights[own_rows, at] = updated.astype(BF16)

    side = 4
    y, z, x, core = me // side, me % side, my // 2, my % 2
    half = block // 2
    strip = half // side
    offsets = (1, 3, 2)

    def move(row, size, send, recv, **peer):
        place = weights.at[pl.ds(pl.multiple_of(row, strip), size)]
        return pltpu.make_async_remote_copy(
            src_ref=place, dst_ref=place, send_sem=send, recv_sem=recv, device_id=peer
        )

    def strip_row(block_index, part, at):
        return block_index * block + part * half + at * strip

    def along_x(k, part, from_x):
        return move(
            strip_row(from_x * 2 + core, part, (y, z)[part]),
            strip,
            x_send.at[k, part],
            x_recv.at[k, part],
            grp=lax.rem(x + k, side) * 2 + core,
        )

    def in_plane(k, part, j, at):
        from_x = lax.rem(x - k + side, side)
        peer = (
            lax.rem(y + j, side) * side + z if part == 0 else y * side + lax.rem(z + j, side)
        )
        return move(
            strip_row(from_x * 2 + core, part, at),
            strip,
            plane_send.at[k, part, j],
            plane_recv.at[k, part, j],
            rep=peer,
        )

    def to_core(k, part, from_core):
        from_x = lax.rem(x - k + side, side)
        return move(
            strip_row(from_x * 2 + from_core, part, 0),
            half,
            core_send.at[k, part],
            core_recv.at[k, part],
            grp=x * 2 + 1 - core,
        )

    for k in offsets:
        for part in (0, 1):
            along_x(k, part, x).start()
    for part in (0, 1):
        to_core(0, part, core).start()
    for start, size in tiles:
        at = slice(start, start + size)
        new_error[:, at] = (grad_in[:, at] + error_in[:, at]) - new_error[:, at]
    for k in offsets:
        for part in (0, 1):
            along_x(k, part, lax.rem(x - k + side, side)).wait_recv()
            for j in offsets:
                in_plane(k, part, j, (y, z)[part]).start()
    for k in offsets:
        for part in (0, 1):
            for j in offsets:
                at = lax.rem((y, z)[part] - j + side, side)
                in_plane(k, part, j, at).wait_recv()
            to_core(k, part, core).start()
    for k in (0,) + offsets:
        for part in (0, 1):
            to_core(k, part, 1 - core).wait_recv()
            to_core(k, part, core).wait_send()
    for k in offsets:
        for part in (0, 1):
            along_x(k, part, x).wait_send()
            for j in offsets:
                in_plane(k, part, j, (y, z)[part]).wait_send()
    for wait in (send_1, send_2, send_3, send_v, send_4, send_5, send_6):
        wait()


def write_kernel(columns, *refs):
    right, momentum, master, gains, error, new_momentum, new_master, weights = refs[:8]
    outs, sems = refs[8:-1], refs[-1]
    query, gate = pl.ds(0, columns), pl.ds(columns, right.shape[1] - columns)
    sources = []
    for whole in (weights, error, new_momentum, new_master, right):
        sources += [whole.at[:, query], whole.at[:, gate]]
    copies = [
        pltpu.make_async_copy(source, out, sems.at[i])
        for i, (source, out) in enumerate(zip(sources + [momentum, master, gains], outs))
    ]
    for copy in copies:
        copy.start()
    for copy in copies:
        copy.wait()


def per_device(
    grad_query,
    error_query,
    basis_query,
    momentum_query,
    master_query,
    grad_gate,
    error_gate,
    basis_gate,
    momentum_gate,
    master_gate,
    vector_grad,
    vector_momentum,
    vector_master,
):
    reps, grps = lax.axis_size("rep"), lax.axis_size("grp")
    grad_query, error_query = grad_query[0], error_query[0]
    grad_gate, error_gate = grad_gate[0], error_gate[0]
    rows, columns = grad_query.shape
    gate = grad_gate.shape[1]
    both = columns + gate
    length = vector_grad.shape[1]
    share = RANK // reps
    any_spec = pl.BlockSpec(memory_space=pl.ANY)
    vmem_spec = pl.BlockSpec(memory_space=VMEM)
    held = (
        ((RANK, both), F32),
        ((1, length), F32),
        ((1, length), F32),
        ((grps * length // 128, 128), BF16),
        ((rows, both), F32),
        ((rows, both), F32),
        ((rows, both), F32),
        ((grps * rows, both), BF16),
    )
    parts = pl.pallas_call(
        functools.partial(factor_kernel, reps, grps),
        out_shape=tuple(VMEM(*entry) for entry in held),
        in_specs=[
            any_spec,
            any_spec,
            vmem_spec,
            any_spec,
            any_spec,
            vmem_spec,
            vmem_spec,
            vmem_spec,
            vmem_spec,
            any_spec,
            any_spec,
            any_spec,
            any_spec,
        ],
        out_specs=[vmem_spec] * len(held),
        scratch_shapes=[
            VMEM((rows, both), F32),
            VMEM((rows, both), F32),
            VMEM((rows, both), F32),
            VMEM((rows, both), F32),
            VMEM((rows, both), BF16),
            VMEM((rows, both), BF16),
            VMEM((reps, 8, rows), F32),
            VMEM((reps, 8, rows), F32),
            VMEM((8, rows), F32),
            VMEM((reps, 8, rows), F32),
            VMEM((BOTH, rows), F32),
            VMEM((grps, RANK // 2, 4 * RANK), F32),
            VMEM((16, 128), F32),
            VMEM((16, 128), BF16),
            VMEM((grps, 16, 128), BF16),
            VMEM((104, 128), F32),
            VMEM((reps, share, both), F32),
            VMEM((reps, share, both), F32),
            VMEM((grps, share, both), F32),
            VMEM((share, both), F32),
            VMEM((reps, share, both), F32),
            pltpu.SemaphoreType.DMA((4, columns // 512 + 1)),
            pltpu.SemaphoreType.DMA((4, reps)),
            pltpu.SemaphoreType.DMA((4, reps)),
            pltpu.SemaphoreType.DMA((3, grps)),
            pltpu.SemaphoreType.DMA((3, grps)),
            pltpu.SemaphoreType.DMA((4, 2)),
            pltpu.SemaphoreType.DMA((4, 2)),
            pltpu.SemaphoreType.DMA((4, 2, 4)),
            pltpu.SemaphoreType.DMA((4, 2, 4)),
            pltpu.SemaphoreType.DMA((4, 2)),
            pltpu.SemaphoreType.DMA((4, 2)),
        ],
        compiler_params=pltpu.CompilerParams(
            collective_id=0, has_side_effects=True, vmem_limit_bytes=40 << 20
        ),
        name="factors",
    )(
        grad_query,
        error_query,
        basis_query.T,
        grad_gate,
        error_gate,
        basis_gate.T,
        vector_grad,
        vector_momentum.reshape(1, length),
        vector_master.reshape(1, length),
        momentum_query,
        master_query,
        momentum_gate,
        master_gate,
    )

    def shapes(row_count, dtype):
        return [
            jax.ShapeDtypeStruct((row_count, columns), dtype),
            jax.ShapeDtypeStruct((row_count, gate), dtype),
        ]

    outs = pl.pallas_call(
        functools.partial(write_kernel, columns),
        out_shape=shapes(grps * rows, BF16)
        + shapes(rows, F32) * 3
        + shapes(RANK, F32)
        + [jax.ShapeDtypeStruct(*entry) for entry in held[1:4]],
        in_specs=[vmem_spec] * len(held),
        out_specs=[any_spec] * 13,
        scratch_shapes=[pltpu.SemaphoreType.DMA((13,))],
        compiler_params=pltpu.CompilerParams(vmem_limit_bytes=8 << 20),
        name="write",
    )(*parts)
    return (
        outs[2][None],
        outs[4],
        outs[6],
        outs[0],
        outs[8].T,
        outs[3][None],
        outs[5],
        outs[7],
        outs[1],
        outs[9].T,
        outs[10].reshape(length),
        outs[11].reshape(length),
        outs[12].reshape(grps * length),
    )


def solution(mesh):
    in_specs = (
        P("rep", "grp", None),
        P("rep", "grp", None),
        P(),
        P("grp", None),
        P("grp", None),
        P("rep", "grp", None),
        P("rep", "grp", None),
        P(),
        P("grp", None),
        P("grp", None),
        P("rep", "grp"),
        P("grp"),
        P("grp"),
    )
    out_specs = (
        P("rep", "grp", None),
        P("grp", None),
        P("grp", None),
        P(),
        P(),
        P("rep", "grp", None),
        P("grp", None),
        P("grp", None),
        P(),
        P(),
        P("grp"),
        P("grp"),
        P(),
    )
    return jax.shard_map(
        per_device, mesh=mesh, in_specs=in_specs, out_specs=out_specs, check_vma=False
    )
```

```python
import functools

import jax
import jax.numpy as jnp
from jax import lax
from jax.experimental import pallas as pl
from jax.experimental.pallas import tpu as pltpu
from jax.sharding import PartitionSpec as P

NS_STEPS = 4
RANK = 32
BOTH = 2 * RANK
HIGHEST = lax.Precision.HIGHEST
F32 = jnp.float32
BF16 = jnp.bfloat16
VMEM = pltpu.VMEM
NT = (((1,), (1,)), ((), ()))


def split(x):
    high = x.astype(BF16)
    return high, (x - high.astype(F32)).astype(BF16)


def mm(a, b, dims=(((1,), (0,)), ((), ()))):
    return lax.dot_general(a, b, dims, preferred_element_type=F32)


def three_pass(a_high, a_low, b_high, b_low, dims=(((1,), (0,)), ((), ()))):
    rows = a_high.shape[0]
    both = mm(jnp.concatenate([a_high, a_low], axis=0), b_high, dims)
    return both[:rows] + both[rows:] + mm(a_high, b_low, dims)


def full_dot(a, b):
    return jnp.dot(a, b, precision=HIGHEST, preferred_element_type=F32)


def inverse_roots(query_gram, gate_gram):
    row = lax.broadcasted_iota(jnp.int32, (BOTH, BOTH), 0)
    column = lax.broadcasted_iota(jnp.int32, (BOTH, BOTH), 1)
    identity = (row == column).astype(F32)
    zero = jnp.zeros((RANK, RANK), F32)
    gram = jnp.concatenate(
        [
            jnp.concatenate([query_gram, zero], axis=1),
            jnp.concatenate([zero, gate_gram], axis=1),
        ],
        axis=0,
    )
    diagonal = jnp.sum(gram * identity, axis=1, keepdims=True)
    is_query = lax.broadcasted_iota(jnp.int32, (BOTH, 1), 0) < RANK
    query_trace = jnp.sum(jnp.where(is_query, diagonal, 0.0), axis=0, keepdims=True)
    gate_trace = jnp.sum(jnp.where(is_query, 0.0, diagonal), axis=0, keepdims=True)
    trace = jnp.where(is_query, query_trace, gate_trace)
    root = gram / trace
    middle = 0.5 * (3.0 * identity - root)
    inverse = middle
    for step in range(1, NS_STEPS):
        root = full_dot(root, middle)
        middle = 0.5 * (3.0 * identity - full_dot(inverse, root))
        inverse = full_dot(middle, inverse)
    return inverse / jnp.sqrt(trace)


def factor_kernel(
    reps,
    grps,
    grad_query,
    error_query,
    basis_query,
    grad_gate,
    error_gate,
    basis_gate,
    vector_grad,
    vector_momentum,
    vector_master,
    momentum_query,
    master_query,
    momentum_gate,
    master_gate,
    right_out,
    momentum_out,
    master_out,
    weight_out,
    new_error,
    new_momentum,
    new_master,
    weights,
    grad_in,
    error_in,
    momentum_in,
    master_in,
    merged_high,
    merged_low,
    left_send,
    left_recv,
    left_sum,
    left_all,
    left,
    gram_all,
    vector_rows,
    vector_send,
    vector_all,
    vector_place,
    right_send,
    right_recv,
    right_part,
    right_final,
    right_all,
    basis_in,
    vector_in,
    first_sem,
    load_sem,
    rep_send,
    rep_recv,
    grp_send,
    grp_recv,
    x_send,
    x_recv,
    plane_send,
    plane_recv,
    core_send,
    core_recv,
):
    me = lax.axis_index("rep")
    my = lax.axis_index("grp")
    columns = grad_query.shape[1]
    gate = grad_gate.shape[1]
    step = 512
    pieces = [(i * step, step, i) for i in range(columns // step)]
    pieces.append((columns, gate, len(pieces)))

    def loads(start, size, index):
        if start < columns:
            grad, error, place = grad_query, error_query, pl.ds(start, size)
        else:
            grad, error, place = grad_gate, error_gate, pl.ds(0, size)
        into = pl.ds(start, size)
        return (
            pltpu.make_async_copy(
                grad.at[:, place], grad_in.at[:, into], load_sem.at[0, index]
            ),
            pltpu.make_async_copy(
                error.at[:, place], error_in.at[:, into], load_sem.at[1, index]
            ),
        )

    first = [
        pltpu.make_async_copy(basis_query, basis_in.at[:, pl.ds(0, columns)], first_sem.at[0]),
        pltpu.make_async_copy(basis_gate, basis_in.at[:, pl.ds(columns, gate)], first_sem.at[1]),
        pltpu.make_async_copy(vector_grad, vector_in, first_sem.at[2]),
    ]
    for copy in first:
        copy.start()
    for piece in pieces:
        for copy in loads(*piece):
            copy.start()

    later = [
        pltpu.make_async_copy(source, into.at[:, at], load_sem.at[2 + i, j])
        for i, (into, pair) in enumerate(
            (
                (momentum_in, (momentum_query, momentum_gate)),
                (master_in, (master_query, master_gate)),
            )
        )
        for j, (source, at) in enumerate(zip(pair, (pl.ds(0, columns), pl.ds(columns, gate))))
    ]
    barrier = pltpu.get_barrier_semaphore()

    def greet_rep(d, carry):
        pl.semaphore_signal(barrier, inc=1, device_id={"rep": lax.rem(me + d, reps)})
        return carry

    def greet_grp(d, carry):
        pl.semaphore_signal(barrier, inc=1, device_id={"grp": lax.rem(my + d, grps)})
        return carry

    lax.fori_loop(1, reps, greet_rep, 0)
    lax.fori_loop(1, grps, greet_grp, 0)

    def to_peers(phase, axis, source, target):
        size, index = (reps, me) if axis == "rep" else (grps, my)
        send, recv = (rep_send, rep_recv) if axis == "rep" else (grp_send, grp_recv)

        def copy(d, at):
            peer = lax.rem(index + d, size)
            return pltpu.make_async_remote_copy(
                src_ref=source(peer),
                dst_ref=target.at[at],
                send_sem=send.at[phase, d],
                recv_sem=recv.at[phase, at],
                device_id={axis: peer},
            )

        def start(d, carry):
            copy(d, index).start()
            return carry

        def await_recv(d, carry):
            copy(d, lax.rem(index + d, size)).wait_recv()
            return carry

        def await_send(d, carry):
            copy(d, index).wait_send()
            return carry

        return (
            lambda: lax.fori_loop(1, size, start, 0),
            lambda: lax.fori_loop(1, size, await_recv, 0),
            lambda: lax.fori_loop(1, size, await_send, 0),
        )

    for copy in first:
        copy.wait()
    left_query = jnp.zeros((RANK, grad_query.shape[0]), F32)
    left_gate = left_query
    for start, size, index in pieces:
        for copy in loads(start, size, index):
            copy.wait()
        at = slice(start, start + size)
        high, low = split(grad_in[:, at] + error_in[:, at])
        merged_high[:, at] = high
        merged_low[:, at] = low
        if start < columns:
            basis = split(basis_in[:, at])
            left_query += three_pass(*basis, high, low, NT)
        else:
            basis = split(basis_in[:, at])
            left_gate += three_pass(*basis, high, low, NT)

    for copy in later:
        copy.start()
    length = vector_grad.shape[1]
    lines = -(-length // 128)
    own = jnp.concatenate([left_query, left_gate], axis=0)
    share = BOTH // reps
    left_send[...] = jnp.zeros_like(left_send)
    for i in range(reps):
        left_send[i, 0:share, :] = own[i * share : (i + 1) * share]
    for i in range(lines):
        width = min(128, length - i * 128)
        left_send[i, share : share + 1, 0:width] = vector_in[:, i * 128 : i * 128 + width]

    pl.semaphore_wait(barrier, reps - 1 + grps - 1)

    start_1, recv_1, send_1 = to_peers(0, "rep", lambda peer: left_send.at[peer], left_recv)
    start_1()
    left_recv[me] = left_send[me]
    recv_1()
    total = left_recv[0]
    for i in range(1, reps):
        total += left_recv[i]
    left_sum[...] = total

    start_2, recv_2, send_2 = to_peers(1, "rep", lambda peer: left_sum, left_all)
    start_2()
    left_all[me] = total
    recv_2()
    for i in range(reps):
        left[i * share : (i + 1) * share, :] = left_all[i, 0:share, :]

    left_high, left_low = split(left[...])
    grams = []
    for part in (slice(0, RANK), slice(RANK, BOTH)):
        grams.append(
            three_pass(left_high[part], left_low[part], left_high[part], left_low[part], NT)
        )
    half = RANK // 2
    gram_all[my] = jnp.concatenate(
        [grams[0][:half], grams[0][half:], grams[1][:half], grams[1][half:]], axis=1
    )
    start_3, recv_3, send_3 = to_peers(0, "grp", lambda peer: gram_all.at[my], gram_all)
    start_3()

    vector_rows[...] = jnp.zeros_like(vector_rows)
    for i in range(lines):
        width = min(128, length - i * 128)
        at = slice(i * 128, i * 128 + width)
        mean = left_all[i, share : share + 1, 0:width] / reps
        gain_momentum = 0.9 * vector_momentum[at].reshape(1, width) + mean
        gain = vector_master[at].reshape(1, width) - 0.5 * gain_momentum
        momentum_out[at] = gain_momentum.reshape(width)
        master_out[at] = gain.reshape(width)
        vector_rows[i : i + 1, 0:width] = gain
    vector_send[...] = vector_rows[...].astype(BF16)
    start_v, recv_v, send_v = to_peers(1, "grp", lambda peer: vector_send, vector_all)
    start_v()
    vector_all[my] = vector_send[...]

    recv_3()
    gram = gram_all[0]
    for i in range(1, grps):
        gram += gram_all[i]
    quarters = [gram[:, i * RANK : (i + 1) * RANK] for i in range(4)]
    query_gram = jnp.concatenate(
        [quarters[0][:, 0:RANK], quarters[1][:, 0:RANK]], axis=0
    )
    gate_gram = jnp.concatenate([quarters[2], quarters[3]], axis=0)
    inverse = inverse_roots(query_gram, gate_gram)
    ortho = full_dot(inverse, left[...])
    ortho_high, ortho_low = split(ortho)

    rows = RANK // reps
    for start, size, index in pieces:
        at = slice(start, start + size)
        part = slice(0, RANK) if start < columns else slice(RANK, BOTH)
        terms = three_pass(
            ortho_high[part], ortho_low[part], merged_high[:, at], merged_low[:, at]
        )
        for i in range(reps):
            right_send[i, :, at] = terms[i * rows : (i + 1) * rows]
    start_4, recv_4, send_4 = to_peers(2, "rep", lambda peer: right_send.at[peer], right_recv)
    start_4()
    right_recv[me] = right_send[me]
    recv_4()
    total = right_recv[0]
    for i in range(1, reps):
        total += right_recv[i]

    right_part[my] = total
    start_5, recv_5, send_5 = to_peers(2, "grp", lambda peer: right_part.at[my], right_part)
    start_5()
    recv_5()
    total = right_part[0]
    for i in range(1, grps):
        total += right_part[i]
    right_final[...] = total

    start_6, recv_6, send_6 = to_peers(3, "rep", lambda peer: right_final, right_all)
    start_6()
    right_all[me] = total

    recv_v()
    low_lanes = lax.broadcasted_iota(jnp.int32, (lines - 1, 128), 1) < 64
    low_lane = lax.broadcasted_iota(jnp.int32, (1, 128), 1) < 64
    for i in range(grps // 2):
        base = i * 2 * length // 128
        even = vector_all[2 * i].astype(F32)
        odd = pltpu.roll(vector_all[2 * i + 1].astype(F32), 64, 1)
        vector_place[base : base + lines - 1, :] = even[: lines - 1]
        vector_place[base + lines - 1 : base + lines, :] = jnp.where(
            low_lane, even[lines - 1 : lines], odd[0:1]
        )
        vector_place[base + lines : base + 2 * lines - 1, :] = jnp.where(
            low_lanes, odd[: lines - 1], odd[1:lines]
        )
    weight_out[...] = vector_place[0 : weight_out.shape[0], :].astype(BF16)

    recv_6()
    for i in range(reps):
        right_out[i * rows : (i + 1) * rows, :] = right_all[i]

    for copy in later:
        copy.wait()
    block = grad_query.shape[0]
    factors = []
    for part in (slice(0, RANK), slice(RANK, BOTH)):
        high, low = split(ortho[part].T / reps)
        factors.append(jnp.concatenate([high, high, low], axis=1))
    own_rows = pl.ds(pl.multiple_of(my * block, block), block)
    tiles = [(start, 256) for start in range(0, columns + gate, 256)]
    for start, size in tiles:
        at = slice(start, start + size)
        high, low = split(right_out[:, at])
        approx = mm(
            factors[0 if start < columns else 1],
            jnp.concatenate([high, low, high], axis=0),
        )
        new_error[:, at] = approx
        moved = 0.9 * momentum_in[:, at] + approx
        new_momentum[:, at] = moved
        updated = master_in[:, at] - 0.5 * moved
        new_master[:, at] = updated
        weights[own_rows, at] = updated.astype(BF16)

    side = 4
    y, z, x, core = me // side, me % side, my // 2, my % 2
    half = block // 2
    strip = half // side

    def move(row, size, send, recv, **peer):
        span = weights.at[pl.ds(pl.multiple_of(row, strip // 2), size)]
        return pltpu.make_async_remote_copy(
            src_ref=span, dst_ref=span, send_sem=send, recv_sem=recv, device_id=peer
        )

    def rows_of(from_x, from_core, part, at):
        return (from_x * 2 + from_core) * block + part * half + at * strip

    def wrap(value):
        return lax.rem(value + 2 * side, side)

    place = (y, z)

    def along_x(k, part, from_x, hop):
        return move(
            rows_of(from_x, core, part, place[part]),
            strip,
            x_send.at[k, part],
            x_recv.at[k, part],
            grp=wrap(x + hop) * 2 + core,
        )

    def in_plane(k, part, j, hop):
        offset = {1: 0, 3: 0, 2: -hop, 0: -hop}[j]
        return strip_move(k, part, j, offset, hop)

    def strip_move(k, part, j, offset, hop):
        row = rows_of(wrap(x - k), core, part, wrap(place[part] + offset))
        size = strip if j in (1, 3) else strip // 2
        if j == 0:
            row += strip // 2
        peer = (
            wrap(y + hop) * side + z if part == 0 else y * side + wrap(z + hop)
        )
        return move(
            row, size, plane_send.at[k, part, j], plane_recv.at[k, part, j], rep=peer
        )

    landed = {1: -1, 3: 1, 2: -2, 0: -2}

    def to_core(k, part, j, from_core):
        row = rows_of(
            wrap(x - k), from_core, part, wrap(place[part] + landed.get(j, 0))
        )
        if j == 0:
            row += strip // 2
        return move(
            row,
            strip // 2 if j in (0, 2) else strip,
            core_send.at[k, part, j],
            core_recv.at[k, part, j],
            grp=x * 2 + 1 - core,
        )

    def own_to_core(part, from_core):
        return move(
            rows_of(x, from_core, part, 0),
            half,
            core_send.at[0, part, 0],
            core_recv.at[0, part, 0],
            grp=x * 2 + 1 - core,
        )

    sends = [along_x(1, 0, x, 1), along_x(3, 1, x, 3), along_x(1, 1, x, 1), along_x(3, 0, x, 3)]
    sends += [own_to_core(0, core), own_to_core(1, core)]
    for copy in sends:
        copy.start()
    for start, size in tiles:
        at = slice(start, start + size)
        new_error[:, at] = (grad_in[:, at] + error_in[:, at]) - new_error[:, at]

    def begin(*copies):
        for copy in copies:
            copy.start()
            sends.append(copy)

    def from_x(k, part):
        along_x(k, part, wrap(x - k), 0).wait_recv()
        if (k, part) in ((1, 0), (3, 1)):
            begin(along_x(2, part, wrap(x - k), k))
        begin(
            in_plane(k, part, 1, 1), in_plane(k, part, 3, 3), to_core(k, part, 4, core)
        )

    def from_neighbours(k, part):
        for j, relayed in ((1, 2), (3, 0)):
            strip_move(k, part, j, landed[j], j).wait_recv()
            begin(in_plane(k, part, relayed, j), to_core(k, part, j, core))

    def from_opposite(k, part):
        for j in (2, 0):
            strip_move(k, part, j, landed[j], 1).wait_recv()
            begin(to_core(k, part, j, core))

    for k, part in ((1, 0), (3, 1), (3, 0), (1, 1)):
        from_x(k, part)
    for k, part in ((1, 0), (3, 1), (3, 0), (1, 1)):
        from_neighbours(k, part)
    for part in (0, 1):
        from_x(2, part)
    for k, part in ((1, 0), (3, 1), (3, 0), (1, 1)):
        from_opposite(k, part)
    for part in (0, 1):
        from_neighbours(2, part)
    for part in (0, 1):
        from_opposite(2, part)
    for part in (0, 1):
        own_to_core(part, 1 - core).wait_recv()
    for k in (1, 3, 2):
        for part in (0, 1):
            for j in range(5):
                to_core(k, part, j, 1 - core).wait_recv()
    for copy in sends:
        copy.wait_send()
    for wait in (send_1, send_2, send_3, send_v, send_4, send_5, send_6):
        wait()


def write_kernel(columns, *refs):
    right, momentum, master, gains, error, new_momentum, new_master, weights = refs[:8]
    outs, sems = refs[8:-1], refs[-1]
    query, gate = pl.ds(0, columns), pl.ds(columns, right.shape[1] - columns)
    sources = []
    for whole in (weights, error, new_momentum, new_master, right):
        sources += [whole.at[:, query], whole.at[:, gate]]
    copies = [
        pltpu.make_async_copy(source, out, sems.at[i])
        for i, (source, out) in enumerate(zip(sources + [momentum, master, gains], outs))
    ]
    for copy in copies:
        copy.start()
    for copy in copies:
        copy.wait()


def per_device(
    grad_query,
    error_query,
    basis_query,
    momentum_query,
    master_query,
    grad_gate,
    error_gate,
    basis_gate,
    momentum_gate,
    master_gate,
    vector_grad,
    vector_momentum,
    vector_master,
):
    reps, grps = lax.axis_size("rep"), lax.axis_size("grp")
    grad_query, error_query = grad_query[0], error_query[0]
    grad_gate, error_gate = grad_gate[0], error_gate[0]
    rows, columns = grad_query.shape
    gate = grad_gate.shape[1]
    both = columns + gate
    length = vector_grad.shape[1]
    share = RANK // reps
    any_spec = pl.BlockSpec(memory_space=pl.ANY)
    vmem_spec = pl.BlockSpec(memory_space=VMEM)
    held = (
        ((RANK, both), F32),
        ((length,), F32),
        ((length,), F32),
        ((grps * length // 128, 128), BF16),
        ((rows, both), F32),
        ((rows, both), F32),
        ((rows, both), F32),
        ((grps * rows, both), BF16),
    )
    parts = pl.pallas_call(
        functools.partial(factor_kernel, reps, grps),
        out_shape=tuple(VMEM(*entry) for entry in held),
        in_specs=[any_spec] * 7 + [vmem_spec] * 2 + [any_spec] * 4,
        out_specs=[vmem_spec] * len(held),
        scratch_shapes=[
            VMEM((rows, both), F32),
            VMEM((rows, both), F32),
            VMEM((rows, both), F32),
            VMEM((rows, both), F32),
            VMEM((rows, both), BF16),
            VMEM((rows, both), BF16),
            VMEM((reps, 8, rows), F32),
            VMEM((reps, 8, rows), F32),
            VMEM((8, rows), F32),
            VMEM((reps, 8, rows), F32),
            VMEM((BOTH, rows), F32),
            VMEM((grps, RANK // 2, 4 * RANK), F32),
            VMEM((16, 128), F32),
            VMEM((16, 128), BF16),
            VMEM((grps, 16, 128), BF16),
            VMEM((104, 128), F32),
            VMEM((reps, share, both), F32),
            VMEM((reps, share, both), F32),
            VMEM((grps, share, both), F32),
            VMEM((share, both), F32),
            VMEM((reps, share, both), F32),
            VMEM((RANK, both), F32),
            VMEM((1, length), F32),
            pltpu.SemaphoreType.DMA((3,)),
            pltpu.SemaphoreType.DMA((4, columns // 512 + 1)),
            pltpu.SemaphoreType.DMA((4, reps)),
            pltpu.SemaphoreType.DMA((4, reps)),
            pltpu.SemaphoreType.DMA((3, grps)),
            pltpu.SemaphoreType.DMA((3, grps)),
            pltpu.SemaphoreType.DMA((4, 2)),
            pltpu.SemaphoreType.DMA((4, 2)),
            pltpu.SemaphoreType.DMA((4, 2, 4)),
            pltpu.SemaphoreType.DMA((4, 2, 4)),
            pltpu.SemaphoreType.DMA((4, 2, 5)),
            pltpu.SemaphoreType.DMA((4, 2, 5)),
        ],
        compiler_params=pltpu.CompilerParams(
            collective_id=0, has_side_effects=True, vmem_limit_bytes=40 << 20
        ),
        name="factors",
    )(
        grad_query,
        error_query,
        basis_query.T,
        grad_gate,
        error_gate,
        basis_gate.T,
        vector_grad,
        vector_momentum,
        vector_master,
        momentum_query,
        master_query,
        momentum_gate,
        master_gate,
    )

    def shapes(row_count, dtype):
        return [
            jax.ShapeDtypeStruct((row_count, columns), dtype),
            jax.ShapeDtypeStruct((row_count, gate), dtype),
        ]

    outs = pl.pallas_call(
        functools.partial(write_kernel, columns),
        out_shape=shapes(grps * rows, BF16)
        + shapes(rows, F32) * 3
        + shapes(RANK, F32)
        + [jax.ShapeDtypeStruct(*entry) for entry in held[1:4]],
        in_specs=[vmem_spec] * len(held),
        out_specs=[any_spec] * 13,
        scratch_shapes=[pltpu.SemaphoreType.DMA((13,))],
        compiler_params=pltpu.CompilerParams(vmem_limit_bytes=8 << 20),
        name="write",
    )(*parts)
    return (
        outs[2][None],
        outs[4],
        outs[6],
        outs[0],
        outs[8].T,
        outs[3][None],
        outs[5],
        outs[7],
        outs[1],
        outs[9].T,
        outs[10],
        outs[11],
        outs[12].reshape(grps * length),
    )


def solution(mesh):
    in_specs = (
        P("rep", "grp", None),
        P("rep", "grp", None),
        P(),
        P("grp", None),
        P("grp", None),
        P("rep", "grp", None),
        P("rep", "grp", None),
        P(),
        P("grp", None),
        P("grp", None),
        P("rep", "grp"),
        P("grp"),
        P("grp"),
    )
    out_specs = (
        P("rep", "grp", None),
        P("grp", None),
        P("grp", None),
        P(),
        P(),
        P("rep", "grp", None),
        P("grp", None),
        P("grp", None),
        P(),
        P(),
        P("grp"),
        P("grp"),
        P(),
    )
    return jax.shard_map(
        per_device, mesh=mesh, in_specs=in_specs, out_specs=out_specs, check_vma=False
    )
```

```python
import functools

import jax
import jax.numpy as jnp
from jax import lax
from jax.experimental import pallas as pl
from jax.experimental.pallas import tpu as pltpu
from jax.sharding import PartitionSpec as P

NS_STEPS = 4
RANK = 32
BOTH = 2 * RANK
HIGHEST = lax.Precision.HIGHEST
F32 = jnp.float32
BF16 = jnp.bfloat16
VMEM = pltpu.VMEM
NT = (((1,), (1,)), ((), ()))


def split(x):
    high = x.astype(BF16)
    return high, (x - high.astype(F32)).astype(BF16)


def mm(a, b, dims=(((1,), (0,)), ((), ()))):
    return lax.dot_general(a, b, dims, preferred_element_type=F32)


def three_pass(a_high, a_low, b_high, b_low, dims=(((1,), (0,)), ((), ()))):
    rows = a_high.shape[0]
    both = mm(jnp.concatenate([a_high, a_low], axis=0), b_high, dims)
    return both[:rows] + both[rows:] + mm(a_high, b_low, dims)


def full_dot(a, b):
    return jnp.dot(a, b, precision=HIGHEST, preferred_element_type=F32)


def inverse_roots(query_gram, gate_gram):
    row = lax.broadcasted_iota(jnp.int32, (BOTH, BOTH), 0)
    column = lax.broadcasted_iota(jnp.int32, (BOTH, BOTH), 1)
    identity = (row == column).astype(F32)
    zero = jnp.zeros((RANK, RANK), F32)
    gram = jnp.concatenate(
        [
            jnp.concatenate([query_gram, zero], axis=1),
            jnp.concatenate([zero, gate_gram], axis=1),
        ],
        axis=0,
    )
    diagonal = jnp.sum(gram * identity, axis=1, keepdims=True)
    is_query = lax.broadcasted_iota(jnp.int32, (BOTH, 1), 0) < RANK
    query_trace = jnp.sum(jnp.where(is_query, diagonal, 0.0), axis=0, keepdims=True)
    gate_trace = jnp.sum(jnp.where(is_query, 0.0, diagonal), axis=0, keepdims=True)
    trace = jnp.where(is_query, query_trace, gate_trace)
    root = gram / trace
    middle = 0.5 * (3.0 * identity - root)
    inverse = middle
    for step in range(1, NS_STEPS):
        root = full_dot(root, middle)
        middle = 0.5 * (3.0 * identity - full_dot(inverse, root))
        inverse = full_dot(middle, inverse)
    return inverse / jnp.sqrt(trace)


def factor_kernel(
    reps,
    grps,
    grad_query,
    error_query,
    basis_query,
    grad_gate,
    error_gate,
    basis_gate,
    vector_grad,
    vector_momentum,
    vector_master,
    momentum_query,
    master_query,
    momentum_gate,
    master_gate,
    right_out,
    momentum_out,
    master_out,
    weight_out,
    new_error,
    new_momentum,
    new_master,
    weights,
    grad_in,
    error_in,
    momentum_in,
    master_in,
    merged_high,
    merged_low,
    left_send,
    left_recv,
    left_sum,
    left_all,
    left,
    gram_all,
    vector_rows,
    vector_send,
    vector_all,
    vector_place,
    right_send,
    right_recv,
    right_part,
    right_final,
    right_all,
    basis_in,
    vector_in,
    base_send,
    base_recv,
    ortho_all,
    factor_all,
    right_cat,
    first_sem,
    load_sem,
    rep_send,
    rep_recv,
    grp_send,
    grp_recv,
    base_sems,
    ortho_sems,
    x_send,
    x_recv,
    far_core_send,
    far_core_recv,
    plane_send,
    plane_recv,
    core_send,
    core_recv,
):
    me = lax.axis_index("rep")
    my = lax.axis_index("grp")
    columns = grad_query.shape[1]
    gate = grad_gate.shape[1]
    step = 512
    pieces = [(i * step, step, i) for i in range(columns // step)]
    pieces.append((columns, gate, len(pieces)))

    def loads(start, size, index):
        if start < columns:
            grad, error, place = grad_query, error_query, pl.ds(start, size)
        else:
            grad, error, place = grad_gate, error_gate, pl.ds(0, size)
        into = pl.ds(start, size)
        return (
            pltpu.make_async_copy(
                grad.at[:, place], grad_in.at[:, into], load_sem.at[0, index]
            ),
            pltpu.make_async_copy(
                error.at[:, place], error_in.at[:, into], load_sem.at[1, index]
            ),
        )

    first = [
        pltpu.make_async_copy(basis_query, basis_in.at[:, pl.ds(0, columns)], first_sem.at[0]),
        pltpu.make_async_copy(basis_gate, basis_in.at[:, pl.ds(columns, gate)], first_sem.at[1]),
        pltpu.make_async_copy(vector_grad, vector_in, first_sem.at[2]),
    ]
    for copy in first:
        copy.start()
    for piece in pieces:
        for copy in loads(*piece):
            copy.start()

    later = [
        pltpu.make_async_copy(source, into.at[:, at], load_sem.at[2 + i, j])
        for i, (into, pair) in enumerate(
            (
                (momentum_in, (momentum_query, momentum_gate)),
                (master_in, (master_query, master_gate)),
            )
        )
        for j, (source, at) in enumerate(zip(pair, (pl.ds(0, columns), pl.ds(columns, gate))))
    ]
    barrier = pltpu.get_barrier_semaphore()

    def greet_rep(d, carry):
        pl.semaphore_signal(barrier, inc=1, device_id={"rep": lax.rem(me + d, reps)})
        return carry

    def greet_grp(d, carry):
        pl.semaphore_signal(barrier, inc=1, device_id={"grp": lax.rem(my + d, grps)})
        return carry

    lax.fori_loop(1, reps, greet_rep, 0)
    lax.fori_loop(1, grps, greet_grp, 0)

    def to_peers(phase, axis, source, target):
        size, index = (reps, me) if axis == "rep" else (grps, my)
        send, recv = (rep_send, rep_recv) if axis == "rep" else (grp_send, grp_recv)

        def copy(d, at):
            peer = lax.rem(index + d, size)
            return pltpu.make_async_remote_copy(
                src_ref=source(peer),
                dst_ref=target.at[at],
                send_sem=send.at[phase, d],
                recv_sem=recv.at[phase, at],
                device_id={axis: peer},
            )

        def start(d, carry):
            copy(d, index).start()
            return carry

        def await_recv(d, carry):
            copy(d, lax.rem(index + d, size)).wait_recv()
            return carry

        def await_send(d, carry):
            copy(d, index).wait_send()
            return carry

        return (
            lambda: lax.fori_loop(1, size, start, 0),
            lambda: lax.fori_loop(1, size, await_recv, 0),
            lambda: lax.fori_loop(1, size, await_send, 0),
        )

    for copy in first:
        copy.wait()
    left_query = jnp.zeros((RANK, grad_query.shape[0]), F32)
    left_gate = left_query
    for start, size, index in pieces:
        for copy in loads(start, size, index):
            copy.wait()
        at = slice(start, start + size)
        high, low = split(grad_in[:, at] + error_in[:, at])
        merged_high[:, at] = high
        merged_low[:, at] = low
        if start < columns:
            basis = split(basis_in[:, at])
            left_query += three_pass(*basis, high, low, NT)
        else:
            basis = split(basis_in[:, at])
            left_gate += three_pass(*basis, high, low, NT)

    for copy in later:
        copy.start()
    length = vector_grad.shape[1]
    lines = -(-length // 128)
    own = jnp.concatenate([left_query, left_gate], axis=0)
    share = BOTH // reps
    left_send[...] = jnp.zeros_like(left_send)
    for i in range(reps):
        left_send[i, 0:share, :] = own[i * share : (i + 1) * share]
    for i in range(lines):
        width = min(128, length - i * 128)
        left_send[i, share : share + 1, 0:width] = vector_in[:, i * 128 : i * 128 + width]

    pl.semaphore_wait(barrier, reps - 1 + grps - 1)

    side = 4
    y, z, x, core = me // side, me % side, my // 2, my % 2
    place = (y, z)
    block = grad_query.shape[0]
    near = block * 3 // 4
    strip = near // side
    rest = block - near
    wide = (columns + gate) // 2
    cut = -(-wide // 256) * 128

    def wrap(value):
        return lax.rem(value + 2 * side, side)

    def send_base(k, part, source, hop):
        return pltpu.make_async_remote_copy(
            src_ref=source,
            dst_ref=base_recv.at[k, part],
            send_sem=base_sems.at[0, k, part],
            recv_sem=base_sems.at[1, k, part],
            device_id={"grp": wrap(x + hop) * 2 + core},
        )

    def send_ortho(k):
        return pltpu.make_async_remote_copy(
            src_ref=ortho_all.at[0],
            dst_ref=ortho_all.at[k],
            send_sem=ortho_sems.at[0, k],
            recv_sem=ortho_sems.at[1, k],
            device_id={"grp": wrap(x + k) * 2 + core},
        )

    sends = []

    def begin(*copies):
        for copy in copies:
            copy.start()
            sends.append(copy)

    start_1, recv_1, send_1 = to_peers(0, "rep", lambda peer: left_send.at[peer], left_recv)
    start_1()
    left_recv[me] = left_send[me]

    for copy in later:
        copy.wait()
    for part in (0, 1):
        at = slice(part * wide, (part + 1) * wide)
        those = pl.ds(pl.multiple_of(place[part] * strip, 16), strip)
        base_send[part] = master_in[those, at] - 0.45 * momentum_in[those, at]
    begin(*[send_base(k, 0, base_send.at[0], k) for k in (1, 3)])
    recv_1()
    total = left_recv[0]
    for i in range(1, reps):
        total += left_recv[i]
    left_sum[...] = total

    start_2, recv_2, send_2 = to_peers(1, "rep", lambda peer: left_sum, left_all)
    start_2()
    left_all[me] = total
    recv_2()
    for i in range(reps):
        left[i * share : (i + 1) * share, :] = left_all[i, 0:share, :]

    left_high, left_low = split(left[...])
    grams = []
    for part in (slice(0, RANK), slice(RANK, BOTH)):
        grams.append(
            three_pass(left_high[part], left_low[part], left_high[part], left_low[part], NT)
        )
    half = RANK // 2
    gram_all[my] = jnp.concatenate(
        [grams[0][:half], grams[0][half:], grams[1][:half], grams[1][half:]], axis=1
    )
    start_3, recv_3, send_3 = to_peers(0, "grp", lambda peer: gram_all.at[my], gram_all)
    start_3()

    vector_rows[...] = jnp.zeros_like(vector_rows)
    for i in range(lines):
        width = min(128, length - i * 128)
        at = slice(i * 128, i * 128 + width)
        mean = left_all[i, share : share + 1, 0:width] / reps
        gain_momentum = 0.9 * vector_momentum[at].reshape(1, width) + mean
        gain = vector_master[at].reshape(1, width) - 0.5 * gain_momentum
        momentum_out[at] = gain_momentum.reshape(width)
        master_out[at] = gain.reshape(width)
        vector_rows[i : i + 1, 0:width] = gain
    vector_send[...] = vector_rows[...].astype(BF16)
    start_v, recv_v, send_v = to_peers(1, "grp", lambda peer: vector_send, vector_all)
    start_v()
    vector_all[my] = vector_send[...]

    recv_3()
    begin(*[send_base(k, 1, base_send.at[1], k) for k in (1, 3)])
    send_base(1, 0, base_send.at[0], 1).wait_recv()
    begin(send_base(2, 0, base_recv.at[1, 0], 1))
    gram = gram_all[0]
    for i in range(1, grps):
        gram += gram_all[i]
    quarters = [gram[:, i * RANK : (i + 1) * RANK] for i in range(4)]
    query_gram = jnp.concatenate(
        [quarters[0][:, 0:RANK], quarters[1][:, 0:RANK]], axis=0
    )
    gate_gram = jnp.concatenate([quarters[2], quarters[3]], axis=0)
    inverse = inverse_roots(query_gram, gate_gram)
    ortho = full_dot(inverse, left[...])
    ortho_all[0] = ortho
    ortho_high, ortho_low = split(ortho)

    rows = RANK // reps
    for start, size, index in pieces:
        at = slice(start, start + size)
        part = slice(0, RANK) if start < columns else slice(RANK, BOTH)
        terms = three_pass(
            ortho_high[part], ortho_low[part], merged_high[:, at], merged_low[:, at]
        )
        for i in range(reps):
            right_send[i, :, at] = terms[i * rows : (i + 1) * rows]
    start_4, recv_4, send_4 = to_peers(2, "rep", lambda peer: right_send.at[peer], right_recv)
    start_4()
    right_recv[me] = right_send[me]
    begin(*[send_ortho(k) for k in (1, 3, 2)])
    send_base(3, 1, base_send.at[1], 3).wait_recv()
    begin(send_base(2, 1, base_recv.at[3, 1], 3))
    recv_4()
    total = right_recv[0]
    for i in range(1, reps):
        total += right_recv[i]

    right_part[my] = total
    start_5, recv_5, send_5 = to_peers(2, "grp", lambda peer: right_part.at[my], right_part)
    start_5()
    recv_5()
    total = right_part[0]
    for i in range(1, grps):
        total += right_part[i]
    right_final[...] = total

    start_6, recv_6, send_6 = to_peers(3, "rep", lambda peer: right_final, right_all)
    start_6()
    right_all[me] = total

    recv_v()
    low_lanes = lax.broadcasted_iota(jnp.int32, (lines - 1, 128), 1) < 64
    low_lane = lax.broadcasted_iota(jnp.int32, (1, 128), 1) < 64
    for i in range(grps // 2):
        base = i * 2 * length // 128
        even = vector_all[2 * i].astype(F32)
        odd = pltpu.roll(vector_all[2 * i + 1].astype(F32), 64, 1)
        vector_place[base : base + lines - 1, :] = even[: lines - 1]
        vector_place[base + lines - 1 : base + lines, :] = jnp.where(
            low_lane, even[lines - 1 : lines], odd[0:1]
        )
        vector_place[base + lines : base + 2 * lines - 1, :] = jnp.where(
            low_lanes, odd[: lines - 1], odd[1:lines]
        )
    weight_out[...] = vector_place[0 : weight_out.shape[0], :].astype(BF16)

    for k in range(side):
        if k:
            send_ortho(k).wait_recv()
        for i in (0, 1):
            high, low = split(ortho_all[k, i * RANK : (i + 1) * RANK].T / reps)
            factor_all[k, i] = jnp.concatenate([high, high, low], axis=1)
    for k, part in ((3, 0), (1, 1), (2, 0), (2, 1)):
        send_base(k, part, base_send.at[part], 1).wait_recv()

    recv_6()
    for i in range(reps):
        right_out[i * rows : (i + 1) * rows, :] = right_all[i]
    for start, size, _ in pieces:
        at = slice(start, start + size)
        high, low = split(right_out[:, at])
        right_cat[:, at] = jnp.concatenate([high, low, high], axis=0)

    own_row = my * block

    def finish(first_row, count):
        those = slice(first_row, first_row + count)
        into = pl.ds(pl.multiple_of(own_row + first_row, 16), count)
        for start in range(0, columns + gate, 256):
            at = slice(start, start + 256)
            approx = mm(
                factor_all[0, 0 if start < columns else 1, those, :], right_cat[:, at]
            )
            new_error[those, at] = approx
            old = momentum_in[those, at]
            new_momentum[those, at] = 0.9 * old + approx
            updated = (master_in[those, at] - 0.45 * old) - 0.5 * approx
            new_master[those, at] = updated
            weights[into, at] = updated.astype(BF16)

    def strip_weights(k, part):
        those = pl.ds(pl.multiple_of(place[part] * strip, 16), strip)
        into = pl.ds(pl.multiple_of(rows_of(wrap(x - k), core, place[part]), 16), strip)
        low, high = part * wide, (part + 1) * wide
        bounds = [(low, min(high, columns), 0), (max(low, columns), high, 1)]
        for start, end, which in bounds:
            if start < end:
                approx = mm(factor_all[k, which, those, :], right_cat[:, start:end])
                base = base_recv[k, part, :, start - low : end - low]
                weights[into, start:end] = (base - 0.5 * approx).astype(BF16)

    def move(row, size, start, width, send, recv, **peer):
        span = weights.at[pl.ds(pl.multiple_of(row, 16), size), pl.ds(start, width)]
        return pltpu.make_async_remote_copy(
            src_ref=span, dst_ref=span, send_sem=send, recv_sem=recv, device_id=peer
        )

    def rows_of(from_x, from_core, at):
        return (from_x * 2 + from_core) * block + at * strip

    def columns_of(part, j):
        low = part * wide
        return {2: (low, cut), 0: (low + cut, wide - cut)}.get(j, (low, wide))

    far = ((1, 0, rest), (3, 0, rest), (2, 0, rest // 2), (2, rest // 2, rest // 2))

    def far_span(slot, from_x, from_core):
        _, offset, size = far[slot]
        return rows_of(from_x, from_core, 0) + near + offset, size, 0, columns + gate

    def along_x(slot, from_x, hop):
        return move(
            *far_span(slot, from_x, core),
            x_send.at[slot],
            x_recv.at[slot],
            grp=wrap(x + hop) * 2 + core,
        )

    def far_to_core(slot, from_core):
        return move(
            *far_span(slot, wrap(x - far[slot][0]), from_core),
            far_core_send.at[slot],
            far_core_recv.at[slot],
            grp=x * 2 + 1 - core,
        )

    def in_plane(k, part, j, hop):
        offset = {1: 0, 3: 0, 2: -hop, 0: -hop}[j]
        return strip_move(k, part, j, offset, hop)

    def strip_move(k, part, j, offset, hop):
        peer = (
            wrap(y + hop) * side + z if part == 0 else y * side + wrap(z + hop)
        )
        return move(
            rows_of(wrap(x - k), core, wrap(place[part] + offset)),
            strip,
            *columns_of(part, j),
            plane_send.at[k, part, j],
            plane_recv.at[k, part, j],
            rep=peer,
        )

    landed = {1: -1, 3: 1, 2: -2, 0: -2}

    def to_core(k, part, j, from_core):
        return move(
            rows_of(wrap(x - k), from_core, wrap(place[part] + landed.get(j, 0))),
            strip,
            *columns_of(part, j),
            core_send.at[k, part, j],
            core_recv.at[k, part, j],
            grp=x * 2 + 1 - core,
        )

    def own_to_core(from_core):
        return move(
            rows_of(x, from_core, 0),
            block,
            0,
            columns + gate,
            core_send.at[0, 0, 0],
            core_recv.at[0, 0, 0],
            grp=x * 2 + 1 - core,
        )

    finish(near, rest)
    begin(along_x(0, x, 1), along_x(1, x, 3))
    order = [(k, part) for k in (1, 3, 2) for part in (0, 1)]
    for k, part in order:
        strip_weights(k, part)
        begin(
            in_plane(k, part, 1, 1), in_plane(k, part, 3, 3), to_core(k, part, 4, core)
        )
    finish(0, near)
    begin(own_to_core(core))

    for slot, hop in ((0, 1), (1, 3)):
        along_x(slot, wrap(x - far[slot][0]), hop).wait_recv()
        begin(along_x(slot + 2, wrap(x - far[slot][0]), hop), far_to_core(slot, core))

    def from_neighbours(k, part):
        for j, relayed in ((1, 2), (3, 0)):
            strip_move(k, part, j, landed[j], j).wait_recv()
            begin(in_plane(k, part, relayed, j), to_core(k, part, j, core))

    def from_opposite(k, part):
        for j in (2, 0):
            strip_move(k, part, j, landed[j], 1).wait_recv()
            begin(to_core(k, part, j, core))

    def errors(start):
        at = slice(start, start + 256)
        new_error[:, at] = (grad_in[:, at] + error_in[:, at]) - new_error[:, at]

    tiles = list(range(0, columns + gate, 256))
    for i, (k, part) in enumerate(order):
        from_neighbours(k, part)
        for start in tiles[i :: len(order)]:
            errors(start)
    for k, part in order:
        from_opposite(k, part)
    for slot in (2, 3):
        along_x(slot, wrap(x - 2), 1).wait_recv()
        begin(far_to_core(slot, core))
    own_to_core(1 - core).wait_recv()
    for slot in range(4):
        far_to_core(slot, 1 - core).wait_recv()
    for k, part in order:
        for j in range(5):
            to_core(k, part, j, 1 - core).wait_recv()
    for copy in sends:
        copy.wait_send()
    for wait in (send_1, send_2, send_3, send_v, send_4, send_5, send_6):
        wait()


def write_kernel(columns, *refs):
    right, momentum, master, gains, error, new_momentum, new_master, weights = refs[:8]
    outs, sems = refs[8:-1], refs[-1]
    query, gate = pl.ds(0, columns), pl.ds(columns, right.shape[1] - columns)
    sources = []
    for whole in (weights, error, new_momentum, new_master, right):
        sources += [whole.at[:, query], whole.at[:, gate]]
    copies = [
        pltpu.make_async_copy(source, out, sems.at[i])
        for i, (source, out) in enumerate(zip(sources + [momentum, master, gains], outs))
    ]
    for copy in copies:
        copy.start()
    for copy in copies:
        copy.wait()


def per_device(
    grad_query,
    error_query,
    basis_query,
    momentum_query,
    master_query,
    grad_gate,
    error_gate,
    basis_gate,
    momentum_gate,
    master_gate,
    vector_grad,
    vector_momentum,
    vector_master,
):
    reps, grps = lax.axis_size("rep"), lax.axis_size("grp")
    grad_query, error_query = grad_query[0], error_query[0]
    grad_gate, error_gate = grad_gate[0], error_gate[0]
    rows, columns = grad_query.shape
    gate = grad_gate.shape[1]
    both = columns + gate
    length = vector_grad.shape[1]
    share = RANK // reps
    any_spec = pl.BlockSpec(memory_space=pl.ANY)
    vmem_spec = pl.BlockSpec(memory_space=VMEM)
    held = (
        ((RANK, both), F32),
        ((length,), F32),
        ((length,), F32),
        ((grps * length // 128, 128), BF16),
        ((rows, both), F32),
        ((rows, both), F32),
        ((rows, both), F32),
        ((grps * rows, both), BF16),
    )
    parts = pl.pallas_call(
        functools.partial(factor_kernel, reps, grps),
        out_shape=tuple(VMEM(*entry) for entry in held),
        in_specs=[any_spec] * 7 + [vmem_spec] * 2 + [any_spec] * 4,
        out_specs=[vmem_spec] * len(held),
        scratch_shapes=[
            VMEM((rows, both), F32),
            VMEM((rows, both), F32),
            VMEM((rows, both), F32),
            VMEM((rows, both), F32),
            VMEM((rows, both), BF16),
            VMEM((rows, both), BF16),
            VMEM((reps, 8, rows), F32),
            VMEM((reps, 8, rows), F32),
            VMEM((8, rows), F32),
            VMEM((reps, 8, rows), F32),
            VMEM((BOTH, rows), F32),
            VMEM((grps, RANK // 2, 4 * RANK), F32),
            VMEM((16, 128), F32),
            VMEM((16, 128), BF16),
            VMEM((grps, 16, 128), BF16),
            VMEM((104, 128), F32),
            VMEM((reps, share, both), F32),
            VMEM((reps, share, both), F32),
            VMEM((grps, share, both), F32),
            VMEM((share, both), F32),
            VMEM((reps, share, both), F32),
            VMEM((RANK, both), F32),
            VMEM((1, length), F32),
            VMEM((2, rows * 3 // 16, both // 2), F32),
            VMEM((4, 2, rows * 3 // 16, both // 2), F32),
            VMEM((4, BOTH, rows), F32),
            VMEM((4, 2, rows, 3 * RANK), BF16),
            VMEM((3 * RANK, both), BF16),
            pltpu.SemaphoreType.DMA((3,)),
            pltpu.SemaphoreType.DMA((4, columns // 512 + 1)),
            pltpu.SemaphoreType.DMA((4, reps)),
            pltpu.SemaphoreType.DMA((4, reps)),
            pltpu.SemaphoreType.DMA((3, grps)),
            pltpu.SemaphoreType.DMA((3, grps)),
            pltpu.SemaphoreType.DMA((2, 4, 2)),
            pltpu.SemaphoreType.DMA((2, 4)),
            pltpu.SemaphoreType.DMA((4,)),
            pltpu.SemaphoreType.DMA((4,)),
            pltpu.SemaphoreType.DMA((4,)),
            pltpu.SemaphoreType.DMA((4,)),
            pltpu.SemaphoreType.DMA((4, 2, 4)),
            pltpu.SemaphoreType.DMA((4, 2, 4)),
            pltpu.SemaphoreType.DMA((4, 2, 5)),
            pltpu.SemaphoreType.DMA((4, 2, 5)),
        ],
        compiler_params=pltpu.CompilerParams(
            collective_id=0, has_side_effects=True, vmem_limit_bytes=40 << 20
        ),
        name="factors",
    )(
        grad_query,
        error_query,
        basis_query.T,
        grad_gate,
        error_gate,
        basis_gate.T,
        vector_grad,
        vector_momentum,
        vector_master,
        momentum_query,
        master_query,
        momentum_gate,
        master_gate,
    )

    def shapes(row_count, dtype):
        return [
            jax.ShapeDtypeStruct((row_count, columns), dtype),
            jax.ShapeDtypeStruct((row_count, gate), dtype),
        ]

    outs = pl.pallas_call(
        functools.partial(write_kernel, columns),
        out_shape=shapes(grps * rows, BF16)
        + shapes(rows, F32) * 3
        + shapes(RANK, F32)
        + [jax.ShapeDtypeStruct(*entry) for entry in held[1:4]],
        in_specs=[vmem_spec] * len(held),
        out_specs=[any_spec] * 13,
        scratch_shapes=[pltpu.SemaphoreType.DMA((13,))],
        compiler_params=pltpu.CompilerParams(vmem_limit_bytes=8 << 20),
        name="write",
    )(*parts)
    return (
        outs[2][None],
        outs[4],
        outs[6],
        outs[0],
        outs[8].T,
        outs[3][None],
        outs[5],
        outs[7],
        outs[1],
        outs[9].T,
        outs[10],
        outs[11],
        outs[12].reshape(grps * length),
    )


def solution(mesh):
    in_specs = (
        P("rep", "grp", None),
        P("rep", "grp", None),
        P(),
        P("grp", None),
        P("grp", None),
        P("rep", "grp", None),
        P("rep", "grp", None),
        P(),
        P("grp", None),
        P("grp", None),
        P("rep", "grp"),
        P("grp"),
        P("grp"),
    )
    out_specs = (
        P("rep", "grp", None),
        P("grp", None),
        P("grp", None),
        P(),
        P(),
        P("rep", "grp", None),
        P("grp", None),
        P("grp", None),
        P(),
        P(),
        P("grp"),
        P("grp"),
        P(),
    )
    return jax.shard_map(
        per_device, mesh=mesh, in_specs=in_specs, out_specs=out_specs, check_vma=False
    )
```

```python
import functools

import jax
import jax.numpy as jnp
from jax import lax
from jax.experimental import pallas as pl
from jax.experimental.pallas import tpu as pltpu
from jax.sharding import PartitionSpec as P

NS_STEPS = 4
RANK = 32
BOTH = 2 * RANK
HIGHEST = lax.Precision.HIGHEST
F32 = jnp.float32
BF16 = jnp.bfloat16
VMEM = pltpu.VMEM
NT = (((1,), (1,)), ((), ()))


def split(x):
    high = x.astype(BF16)
    return high, (x - high.astype(F32)).astype(BF16)


def mm(a, b, dims=(((1,), (0,)), ((), ()))):
    return lax.dot_general(a, b, dims, preferred_element_type=F32)


def three_pass(a_high, a_low, b_high, b_low, dims=(((1,), (0,)), ((), ()))):
    rows = a_high.shape[0]
    both = mm(jnp.concatenate([a_high, a_low], axis=0), b_high, dims)
    return both[:rows] + both[rows:] + mm(a_high, b_low, dims)


def full_dot(a, b):
    return jnp.dot(a, b, precision=HIGHEST, preferred_element_type=F32)


def inverse_roots(query_gram, gate_gram):
    row = lax.broadcasted_iota(jnp.int32, (BOTH, BOTH), 0)
    column = lax.broadcasted_iota(jnp.int32, (BOTH, BOTH), 1)
    identity = (row == column).astype(F32)
    zero = jnp.zeros((RANK, RANK), F32)
    gram = jnp.concatenate(
        [
            jnp.concatenate([query_gram, zero], axis=1),
            jnp.concatenate([zero, gate_gram], axis=1),
        ],
        axis=0,
    )
    diagonal = jnp.sum(gram * identity, axis=1, keepdims=True)
    is_query = lax.broadcasted_iota(jnp.int32, (BOTH, 1), 0) < RANK
    query_trace = jnp.sum(jnp.where(is_query, diagonal, 0.0), axis=0, keepdims=True)
    gate_trace = jnp.sum(jnp.where(is_query, 0.0, diagonal), axis=0, keepdims=True)
    trace = jnp.where(is_query, query_trace, gate_trace)
    root = gram / trace
    middle = 0.5 * (3.0 * identity - root)
    inverse = middle
    for step in range(1, NS_STEPS):
        root = full_dot(root, middle)
        middle = 0.5 * (3.0 * identity - full_dot(inverse, root))
        inverse = full_dot(middle, inverse)
    return inverse / jnp.sqrt(trace)


def factor_kernel(
    reps,
    grps,
    grad_query,
    error_query,
    basis_query,
    grad_gate,
    error_gate,
    basis_gate,
    vector_grad,
    vector_momentum,
    vector_master,
    momentum_query,
    master_query,
    momentum_gate,
    master_gate,
    right_out,
    momentum_out,
    master_out,
    weight_out,
    new_error,
    new_momentum,
    new_master,
    weights,
    grad_in,
    error_in,
    momentum_in,
    master_in,
    merged_high,
    merged_low,
    left_send,
    left_recv,
    left_sum,
    left_all,
    left,
    gram_all,
    vector_rows,
    vector_send,
    vector_all,
    vector_place,
    right_send,
    right_recv,
    right_part,
    right_final,
    right_all,
    basis_in,
    vector_in,
    base_in,
    base_send,
    base_recv,
    ortho_all,
    factor_all,
    right_cat,
    first_sem,
    load_sem,
    rep_send,
    rep_recv,
    grp_send,
    grp_recv,
    strip_sems,
    base_sems,
    ortho_sems,
    x_send,
    x_recv,
    far_core_send,
    far_core_recv,
    plane_send,
    plane_recv,
    core_send,
    core_recv,
):
    me = lax.axis_index("rep")
    my = lax.axis_index("grp")
    columns = grad_query.shape[1]
    gate = grad_gate.shape[1]
    step = 512
    pieces = [(i * step, step, i) for i in range(columns // step)]
    pieces.append((columns, gate, len(pieces)))

    def loads(start, size, index):
        if start < columns:
            grad, error, place = grad_query, error_query, pl.ds(start, size)
        else:
            grad, error, place = grad_gate, error_gate, pl.ds(0, size)
        into = pl.ds(start, size)
        return (
            pltpu.make_async_copy(
                grad.at[:, place], grad_in.at[:, into], load_sem.at[0, index]
            ),
            pltpu.make_async_copy(
                error.at[:, place], error_in.at[:, into], load_sem.at[1, index]
            ),
        )

    side = 4
    y, z, x, core = me // side, me % side, my // 2, my % 2
    place = (y, z)
    block = grad_query.shape[0]
    near = block * 3 // 4
    strip = near // side
    rest = block - near
    wide = (columns + gate) // 2
    cut = -(-wide // 256) * 128

    def wrap(value):
        return lax.rem(value + 2 * side, side)

    def send_base(k, part, source, hop):
        return pltpu.make_async_remote_copy(
            src_ref=source,
            dst_ref=base_recv.at[k, part],
            send_sem=base_sems.at[0, k, part],
            recv_sem=base_sems.at[1, k, part],
            device_id={"grp": wrap(x + hop) * 2 + core},
        )

    def send_ortho(k):
        return pltpu.make_async_remote_copy(
            src_ref=ortho_all.at[0],
            dst_ref=ortho_all.at[k],
            send_sem=ortho_sems.at[0, k],
            recv_sem=ortho_sems.at[1, k],
            device_id={"grp": wrap(x + k) * 2 + core},
        )

    sends = []

    def begin(*copies):
        for copy in copies:
            copy.start()
            sends.append(copy)

    strips = []
    for part in (0, 1):
        those = pl.ds(pl.multiple_of(place[part] * strip, 16), strip)
        low, high = part * wide, (part + 1) * wide
        for i, pair in enumerate(
            ((momentum_query, momentum_gate), (master_query, master_gate))
        ):
            for j, (start, end) in enumerate(
                ((low, min(high, columns)), (max(low, columns), high))
            ):
                if start < end:
                    strips.append(
                        pltpu.make_async_copy(
                            pair[j].at[those, pl.ds(start - j * columns, end - start)],
                            base_in.at[part, i, :, pl.ds(start - low, end - start)],
                            strip_sems.at[part, i, j],
                        )
                    )
    for copy in strips:
        copy.start()

    first = [
        pltpu.make_async_copy(basis_query, basis_in.at[:, pl.ds(0, columns)], first_sem.at[0]),
        pltpu.make_async_copy(basis_gate, basis_in.at[:, pl.ds(columns, gate)], first_sem.at[1]),
        pltpu.make_async_copy(vector_grad, vector_in, first_sem.at[2]),
    ]
    for copy in first:
        copy.start()
    for piece in pieces:
        for copy in loads(*piece):
            copy.start()

    later = [
        pltpu.make_async_copy(source, into.at[:, at], load_sem.at[2 + i, j])
        for i, (into, pair) in enumerate(
            (
                (momentum_in, (momentum_query, momentum_gate)),
                (master_in, (master_query, master_gate)),
            )
        )
        for j, (source, at) in enumerate(zip(pair, (pl.ds(0, columns), pl.ds(columns, gate))))
    ]
    barrier = pltpu.get_barrier_semaphore()

    def greet_rep(d, carry):
        pl.semaphore_signal(barrier, inc=1, device_id={"rep": lax.rem(me + d, reps)})
        return carry

    def greet_grp(d, carry):
        pl.semaphore_signal(barrier, inc=1, device_id={"grp": lax.rem(my + d, grps)})
        return carry

    lax.fori_loop(1, reps, greet_rep, 0)
    lax.fori_loop(1, grps, greet_grp, 0)

    def to_peers(phase, axis, source, target):
        size, index = (reps, me) if axis == "rep" else (grps, my)
        send, recv = (rep_send, rep_recv) if axis == "rep" else (grp_send, grp_recv)

        def copy(d, at):
            peer = lax.rem(index + d, size)
            return pltpu.make_async_remote_copy(
                src_ref=source(peer),
                dst_ref=target.at[at],
                send_sem=send.at[phase, d],
                recv_sem=recv.at[phase, at],
                device_id={axis: peer},
            )

        def start(d, carry):
            copy(d, index).start()
            return carry

        def await_recv(d, carry):
            copy(d, lax.rem(index + d, size)).wait_recv()
            return carry

        def await_send(d, carry):
            copy(d, index).wait_send()
            return carry

        return (
            lambda: lax.fori_loop(1, size, start, 0),
            lambda: lax.fori_loop(1, size, await_recv, 0),
            lambda: lax.fori_loop(1, size, await_send, 0),
        )

    for copy in first:
        copy.wait()
    left_query = jnp.zeros((RANK, grad_query.shape[0]), F32)
    left_gate = left_query
    for start, size, index in pieces:
        if index == 1:
            for copy in strips:
                copy.wait()
            for part in (0, 1):
                base_send[part] = base_in[part, 1] - 0.45 * base_in[part, 0]
            pl.semaphore_wait(barrier, reps - 1 + grps - 1)
            for k, part in ((1, 0), (3, 1), (3, 0), (1, 1)):
                begin(send_base(k, part, base_send.at[part], k))
        for copy in loads(start, size, index):
            copy.wait()
        at = slice(start, start + size)
        high, low = split(grad_in[:, at] + error_in[:, at])
        merged_high[:, at] = high
        merged_low[:, at] = low
        if start < columns:
            basis = split(basis_in[:, at])
            left_query += three_pass(*basis, high, low, NT)
        else:
            basis = split(basis_in[:, at])
            left_gate += three_pass(*basis, high, low, NT)

    for copy in later:
        copy.start()
    length = vector_grad.shape[1]
    lines = -(-length // 128)
    own = jnp.concatenate([left_query, left_gate], axis=0)
    share = BOTH // reps
    left_send[...] = jnp.zeros_like(left_send)
    for i in range(reps):
        left_send[i, 0:share, :] = own[i * share : (i + 1) * share]
    for i in range(lines):
        width = min(128, length - i * 128)
        left_send[i, share : share + 1, 0:width] = vector_in[:, i * 128 : i * 128 + width]

    start_1, recv_1, send_1 = to_peers(0, "rep", lambda peer: left_send.at[peer], left_recv)
    start_1()
    left_recv[me] = left_send[me]
    recv_1()
    total = left_recv[0]
    for i in range(1, reps):
        total += left_recv[i]
    left_sum[...] = total


    start_2, recv_2, send_2 = to_peers(1, "rep", lambda peer: left_sum, left_all)
    start_2()
    left_all[me] = total
    recv_2()
    for i in range(reps):
        left[i * share : (i + 1) * share, :] = left_all[i, 0:share, :]

    left_high, left_low = split(left[...])
    grams = []
    for part in (slice(0, RANK), slice(RANK, BOTH)):
        grams.append(
            three_pass(left_high[part], left_low[part], left_high[part], left_low[part], NT)
        )
    half = RANK // 2
    gram_all[my] = jnp.concatenate(
        [grams[0][:half], grams[0][half:], grams[1][:half], grams[1][half:]], axis=1
    )
    start_3, recv_3, send_3 = to_peers(0, "grp", lambda peer: gram_all.at[my], gram_all)
    start_3()

    vector_rows[...] = jnp.zeros_like(vector_rows)
    for i in range(lines):
        width = min(128, length - i * 128)
        at = slice(i * 128, i * 128 + width)
        mean = left_all[i, share : share + 1, 0:width] / reps
        gain_momentum = 0.9 * vector_momentum[at].reshape(1, width) + mean
        gain = vector_master[at].reshape(1, width) - 0.5 * gain_momentum
        momentum_out[at] = gain_momentum.reshape(width)
        master_out[at] = gain.reshape(width)
        vector_rows[i : i + 1, 0:width] = gain
    vector_send[...] = vector_rows[...].astype(BF16)
    start_v, recv_v, send_v = to_peers(1, "grp", lambda peer: vector_send, vector_all)
    start_v()
    vector_all[my] = vector_send[...]

    recv_3()
    for k, part in ((1, 0), (3, 1)):
        send_base(k, part, base_send.at[part], k).wait_recv()
        begin(send_base(2, part, base_recv.at[k, part], k))
    gram = gram_all[0]
    for i in range(1, grps):
        gram += gram_all[i]
    quarters = [gram[:, i * RANK : (i + 1) * RANK] for i in range(4)]
    query_gram = jnp.concatenate(
        [quarters[0][:, 0:RANK], quarters[1][:, 0:RANK]], axis=0
    )
    gate_gram = jnp.concatenate([quarters[2], quarters[3]], axis=0)
    inverse = inverse_roots(query_gram, gate_gram)
    ortho = full_dot(inverse, left[...])
    ortho_all[0] = ortho
    ortho_high, ortho_low = split(ortho)

    rows = RANK // reps
    for start, size, index in pieces:
        at = slice(start, start + size)
        part = slice(0, RANK) if start < columns else slice(RANK, BOTH)
        terms = three_pass(
            ortho_high[part], ortho_low[part], merged_high[:, at], merged_low[:, at]
        )
        for i in range(reps):
            right_send[i, :, at] = terms[i * rows : (i + 1) * rows]
    start_4, recv_4, send_4 = to_peers(2, "rep", lambda peer: right_send.at[peer], right_recv)
    start_4()
    right_recv[me] = right_send[me]
    begin(*[send_ortho(k) for k in (1, 3, 2)])
    recv_4()
    total = right_recv[0]
    for i in range(1, reps):
        total += right_recv[i]

    right_part[my] = total
    start_5, recv_5, send_5 = to_peers(2, "grp", lambda peer: right_part.at[my], right_part)
    start_5()
    recv_5()
    total = right_part[0]
    for i in range(1, grps):
        total += right_part[i]
    right_final[...] = total

    start_6, recv_6, send_6 = to_peers(3, "rep", lambda peer: right_final, right_all)
    start_6()
    right_all[me] = total

    recv_v()
    low_lanes = lax.broadcasted_iota(jnp.int32, (lines - 1, 128), 1) < 64
    low_lane = lax.broadcasted_iota(jnp.int32, (1, 128), 1) < 64
    for i in range(grps // 2):
        base = i * 2 * length // 128
        even = vector_all[2 * i].astype(F32)
        odd = pltpu.roll(vector_all[2 * i + 1].astype(F32), 64, 1)
        vector_place[base : base + lines - 1, :] = even[: lines - 1]
        vector_place[base + lines - 1 : base + lines, :] = jnp.where(
            low_lane, even[lines - 1 : lines], odd[0:1]
        )
        vector_place[base + lines : base + 2 * lines - 1, :] = jnp.where(
            low_lanes, odd[: lines - 1], odd[1:lines]
        )
    weight_out[...] = vector_place[0 : weight_out.shape[0], :].astype(BF16)

    for k in range(side):
        if k:
            send_ortho(k).wait_recv()
        for i in (0, 1):
            high, low = split(ortho_all[k, i * RANK : (i + 1) * RANK].T / reps)
            factor_all[k, i] = jnp.concatenate([high, high, low], axis=1)
    for k, part in ((3, 0), (1, 1), (2, 0), (2, 1)):
        send_base(k, part, base_send.at[part], 1).wait_recv()

    for copy in later:
        copy.wait()
    recv_6()
    for i in range(reps):
        right_out[i * rows : (i + 1) * rows, :] = right_all[i]
    for start, size, _ in pieces:
        at = slice(start, start + size)
        high, low = split(right_out[:, at])
        right_cat[:, at] = jnp.concatenate([high, low, high], axis=0)

    own_row = my * block

    def finish(first_row, count):
        those = slice(first_row, first_row + count)
        into = pl.ds(pl.multiple_of(own_row + first_row, 16), count)
        for start in range(0, columns + gate, 256):
            at = slice(start, start + 256)
            approx = mm(
                factor_all[0, 0 if start < columns else 1, those, :], right_cat[:, at]
            )
            new_error[those, at] = approx
            old = momentum_in[those, at]
            new_momentum[those, at] = 0.9 * old + approx
            updated = (master_in[those, at] - 0.45 * old) - 0.5 * approx
            new_master[those, at] = updated
            weights[into, at] = updated.astype(BF16)

    def strip_weights(k, part):
        those = pl.ds(pl.multiple_of(place[part] * strip, 16), strip)
        into = pl.ds(pl.multiple_of(rows_of(wrap(x - k), core, place[part]), 16), strip)
        low, high = part * wide, (part + 1) * wide
        bounds = [(low, min(high, columns), 0), (max(low, columns), high, 1)]
        for start, end, which in bounds:
            if start < end:
                approx = mm(factor_all[k, which, those, :], right_cat[:, start:end])
                base = base_recv[k, part, :, start - low : end - low]
                weights[into, start:end] = (base - 0.5 * approx).astype(BF16)

    def move(row, size, start, width, send, recv, **peer):
        span = weights.at[pl.ds(pl.multiple_of(row, 16), size), pl.ds(start, width)]
        return pltpu.make_async_remote_copy(
            src_ref=span, dst_ref=span, send_sem=send, recv_sem=recv, device_id=peer
        )

    def rows_of(from_x, from_core, at):
        return (from_x * 2 + from_core) * block + at * strip

    def columns_of(part, j):
        low = part * wide
        return {2: (low, cut), 0: (low + cut, wide - cut)}.get(j, (low, wide))

    far = ((1, 0, rest), (3, 0, rest), (2, 0, rest // 2), (2, rest // 2, rest // 2))

    def far_span(slot, from_x, from_core):
        _, offset, size = far[slot]
        return rows_of(from_x, from_core, 0) + near + offset, size, 0, columns + gate

    def along_x(slot, from_x, hop):
        return move(
            *far_span(slot, from_x, core),
            x_send.at[slot],
            x_recv.at[slot],
            grp=wrap(x + hop) * 2 + core,
        )

    def far_to_core(slot, from_core):
        return move(
            *far_span(slot, wrap(x - far[slot][0]), from_core),
            far_core_send.at[slot],
            far_core_recv.at[slot],
            grp=x * 2 + 1 - core,
        )

    def in_plane(k, part, j, hop):
        offset = {1: 0, 3: 0, 2: -hop, 0: -hop}[j]
        return strip_move(k, part, j, offset, hop)

    def strip_move(k, part, j, offset, hop):
        peer = (
            wrap(y + hop) * side + z if part == 0 else y * side + wrap(z + hop)
        )
        return move(
            rows_of(wrap(x - k), core, wrap(place[part] + offset)),
            strip,
            *columns_of(part, j),
            plane_send.at[k, part, j],
            plane_recv.at[k, part, j],
            rep=peer,
        )

    landed = {1: -1, 3: 1, 2: -2, 0: -2}

    def to_core(k, part, j, from_core):
        return move(
            rows_of(wrap(x - k), from_core, wrap(place[part] + landed.get(j, 0))),
            strip,
            *columns_of(part, j),
            core_send.at[k, part, j],
            core_recv.at[k, part, j],
            grp=x * 2 + 1 - core,
        )

    def own_to_core(from_core):
        return move(
            rows_of(x, from_core, 0),
            block,
            0,
            columns + gate,
            core_send.at[0, 0, 0],
            core_recv.at[0, 0, 0],
            grp=x * 2 + 1 - core,
        )

    finish(near, rest)
    begin(along_x(0, x, 1), along_x(1, x, 3))
    order = [(k, part) for k in (1, 3, 2) for part in (0, 1)]
    for k, part in order:
        strip_weights(k, part)
        begin(
            in_plane(k, part, 1, 1), in_plane(k, part, 3, 3), to_core(k, part, 4, core)
        )
    finish(0, near)
    begin(own_to_core(core))

    for slot, hop in ((0, 1), (1, 3)):
        along_x(slot, wrap(x - far[slot][0]), hop).wait_recv()
        begin(along_x(slot + 2, wrap(x - far[slot][0]), hop), far_to_core(slot, core))

    def from_neighbours(k, part):
        for j, relayed in ((1, 2), (3, 0)):
            strip_move(k, part, j, landed[j], j).wait_recv()
            begin(in_plane(k, part, relayed, j), to_core(k, part, j, core))

    def from_opposite(k, part):
        for j in (2, 0):
            strip_move(k, part, j, landed[j], 1).wait_recv()
            begin(to_core(k, part, j, core))

    def errors(start):
        at = slice(start, start + 256)
        new_error[:, at] = (grad_in[:, at] + error_in[:, at]) - new_error[:, at]

    tiles = list(range(0, columns + gate, 256))
    for i, (k, part) in enumerate(order):
        from_neighbours(k, part)
        for start in tiles[i :: len(order)]:
            errors(start)
    for k, part in order:
        from_opposite(k, part)
    for slot in (2, 3):
        along_x(slot, wrap(x - 2), 1).wait_recv()
        begin(far_to_core(slot, core))
    own_to_core(1 - core).wait_recv()
    for slot in range(4):
        far_to_core(slot, 1 - core).wait_recv()
    for k, part in order:
        for j in range(5):
            to_core(k, part, j, 1 - core).wait_recv()
    for copy in sends:
        copy.wait_send()
    for wait in (send_1, send_2, send_3, send_v, send_4, send_5, send_6):
        wait()


def write_kernel(columns, *refs):
    right, momentum, master, gains, error, new_momentum, new_master, weights = refs[:8]
    outs, sems = refs[8:-1], refs[-1]
    query, gate = pl.ds(0, columns), pl.ds(columns, right.shape[1] - columns)
    sources = []
    for whole in (weights, error, new_momentum, new_master, right):
        sources += [whole.at[:, query], whole.at[:, gate]]
    copies = [
        pltpu.make_async_copy(source, out, sems.at[i])
        for i, (source, out) in enumerate(zip(sources + [momentum, master, gains], outs))
    ]
    for copy in copies:
        copy.start()
    for copy in copies:
        copy.wait()


def per_device(
    grad_query,
    error_query,
    basis_query,
    momentum_query,
    master_query,
    grad_gate,
    error_gate,
    basis_gate,
    momentum_gate,
    master_gate,
    vector_grad,
    vector_momentum,
    vector_master,
):
    reps, grps = lax.axis_size("rep"), lax.axis_size("grp")
    grad_query, error_query = grad_query[0], error_query[0]
    grad_gate, error_gate = grad_gate[0], error_gate[0]
    rows, columns = grad_query.shape
    gate = grad_gate.shape[1]
    both = columns + gate
    length = vector_grad.shape[1]
    share = RANK // reps
    any_spec = pl.BlockSpec(memory_space=pl.ANY)
    vmem_spec = pl.BlockSpec(memory_space=VMEM)
    held = (
        ((RANK, both), F32),
        ((length,), F32),
        ((length,), F32),
        ((grps * length // 128, 128), BF16),
        ((rows, both), F32),
        ((rows, both), F32),
        ((rows, both), F32),
        ((grps * rows, both), BF16),
    )
    parts = pl.pallas_call(
        functools.partial(factor_kernel, reps, grps),
        out_shape=tuple(VMEM(*entry) for entry in held),
        in_specs=[any_spec] * 7 + [vmem_spec] * 2 + [any_spec] * 4,
        out_specs=[vmem_spec] * len(held),
        scratch_shapes=[
            VMEM((rows, both), F32),
            VMEM((rows, both), F32),
            VMEM((rows, both), F32),
            VMEM((rows, both), F32),
            VMEM((rows, both), BF16),
            VMEM((rows, both), BF16),
            VMEM((reps, 8, rows), F32),
            VMEM((reps, 8, rows), F32),
            VMEM((8, rows), F32),
            VMEM((reps, 8, rows), F32),
            VMEM((BOTH, rows), F32),
            VMEM((grps, RANK // 2, 4 * RANK), F32),
            VMEM((16, 128), F32),
            VMEM((16, 128), BF16),
            VMEM((grps, 16, 128), BF16),
            VMEM((104, 128), F32),
            VMEM((reps, share, both), F32),
            VMEM((reps, share, both), F32),
            VMEM((grps, share, both), F32),
            VMEM((share, both), F32),
            VMEM((reps, share, both), F32),
            VMEM((RANK, both), F32),
            VMEM((1, length), F32),
            VMEM((2, 2, rows * 3 // 16, both // 2), F32),
            VMEM((2, rows * 3 // 16, both // 2), F32),
            VMEM((4, 2, rows * 3 // 16, both // 2), F32),
            VMEM((4, BOTH, rows), F32),
            VMEM((4, 2, rows, 3 * RANK), BF16),
            VMEM((3 * RANK, both), BF16),
            pltpu.SemaphoreType.DMA((3,)),
            pltpu.SemaphoreType.DMA((4, columns // 512 + 1)),
            pltpu.SemaphoreType.DMA((4, reps)),
            pltpu.SemaphoreType.DMA((4, reps)),
            pltpu.SemaphoreType.DMA((3, grps)),
            pltpu.SemaphoreType.DMA((3, grps)),
            pltpu.SemaphoreType.DMA((2, 2, 2)),
            pltpu.SemaphoreType.DMA((2, 4, 2)),
            pltpu.SemaphoreType.DMA((2, 4)),
            pltpu.SemaphoreType.DMA((4,)),
            pltpu.SemaphoreType.DMA((4,)),
            pltpu.SemaphoreType.DMA((4,)),
            pltpu.SemaphoreType.DMA((4,)),
            pltpu.SemaphoreType.DMA((4, 2, 4)),
            pltpu.SemaphoreType.DMA((4, 2, 4)),
            pltpu.SemaphoreType.DMA((4, 2, 5)),
            pltpu.SemaphoreType.DMA((4, 2, 5)),
        ],
        compiler_params=pltpu.CompilerParams(
            collective_id=0, has_side_effects=True, vmem_limit_bytes=40 << 20
        ),
        name="factors",
    )(
        grad_query,
        error_query,
        basis_query.T,
        grad_gate,
        error_gate,
        basis_gate.T,
        vector_grad,
        vector_momentum,
        vector_master,
        momentum_query,
        master_query,
        momentum_gate,
        master_gate,
    )

    def shapes(row_count, dtype):
        return [
            jax.ShapeDtypeStruct((row_count, columns), dtype),
            jax.ShapeDtypeStruct((row_count, gate), dtype),
        ]

    outs = pl.pallas_call(
        functools.partial(write_kernel, columns),
        out_shape=shapes(grps * rows, BF16)
        + shapes(rows, F32) * 3
        + shapes(RANK, F32)
        + [jax.ShapeDtypeStruct(*entry) for entry in held[1:4]],
        in_specs=[vmem_spec] * len(held),
        out_specs=[any_spec] * 13,
        scratch_shapes=[pltpu.SemaphoreType.DMA((13,))],
        compiler_params=pltpu.CompilerParams(vmem_limit_bytes=8 << 20),
        name="write",
    )(*parts)
    return (
        outs[2][None],
        outs[4],
        outs[6],
        outs[0],
        outs[8].T,
        outs[3][None],
        outs[5],
        outs[7],
        outs[1],
        outs[9].T,
        outs[10],
        outs[11],
        outs[12].reshape(grps * length),
    )


def solution(mesh):
    in_specs = (
        P("rep", "grp", None),
        P("rep", "grp", None),
        P(),
        P("grp", None),
        P("grp", None),
        P("rep", "grp", None),
        P("rep", "grp", None),
        P(),
        P("grp", None),
        P("grp", None),
        P("rep", "grp"),
        P("grp"),
        P("grp"),
    )
    out_specs = (
        P("rep", "grp", None),
        P("grp", None),
        P("grp", None),
        P(),
        P(),
        P("rep", "grp", None),
        P("grp", None),
        P("grp", None),
        P(),
        P(),
        P("grp"),
        P("grp"),
        P(),
    )
    return jax.shard_map(
        per_device, mesh=mesh, in_specs=in_specs, out_specs=out_specs, check_vma=False
    )
```

```python
import functools

import jax
import jax.numpy as jnp
from jax import lax
from jax.experimental import pallas as pl
from jax.experimental.pallas import tpu as pltpu
from jax.sharding import PartitionSpec as P

NS_STEPS = 4
RANK = 32
BOTH = 2 * RANK
HIGHEST = lax.Precision.HIGHEST
F32 = jnp.float32
BF16 = jnp.bfloat16
VMEM = pltpu.VMEM
NT = (((1,), (1,)), ((), ()))


def split(x):
    high = x.astype(BF16)
    return high, (x - high.astype(F32)).astype(BF16)


def mm(a, b, dims=(((1,), (0,)), ((), ()))):
    return lax.dot_general(a, b, dims, preferred_element_type=F32)


def three_pass(a_high, a_low, b_high, b_low, dims=(((1,), (0,)), ((), ()))):
    rows = a_high.shape[0]
    both = mm(jnp.concatenate([a_high, a_low], axis=0), b_high, dims)
    return both[:rows] + both[rows:] + mm(a_high, b_low, dims)


def full_dot(a, b):
    return jnp.dot(a, b, precision=HIGHEST, preferred_element_type=F32)


def inverse_roots(query_gram, gate_gram):
    row = lax.broadcasted_iota(jnp.int32, (BOTH, BOTH), 0)
    column = lax.broadcasted_iota(jnp.int32, (BOTH, BOTH), 1)
    identity = (row == column).astype(F32)
    zero = jnp.zeros((RANK, RANK), F32)
    gram = jnp.concatenate(
        [
            jnp.concatenate([query_gram, zero], axis=1),
            jnp.concatenate([zero, gate_gram], axis=1),
        ],
        axis=0,
    )
    diagonal = jnp.sum(gram * identity, axis=1, keepdims=True)
    is_query = lax.broadcasted_iota(jnp.int32, (BOTH, 1), 0) < RANK
    query_trace = jnp.sum(jnp.where(is_query, diagonal, 0.0), axis=0, keepdims=True)
    gate_trace = jnp.sum(jnp.where(is_query, 0.0, diagonal), axis=0, keepdims=True)
    trace = jnp.where(is_query, query_trace, gate_trace)
    root = gram / trace
    middle = 0.5 * (3.0 * identity - root)
    inverse = middle
    for step in range(1, NS_STEPS):
        root = full_dot(root, middle)
        middle = 0.5 * (3.0 * identity - full_dot(inverse, root))
        inverse = full_dot(middle, inverse)
    return inverse / jnp.sqrt(trace)


def factor_kernel(
    reps,
    grps,
    grad_query,
    error_query,
    basis_query,
    grad_gate,
    error_gate,
    basis_gate,
    vector_grad,
    vector_momentum,
    vector_master,
    momentum_query,
    master_query,
    momentum_gate,
    master_gate,
    right_out,
    momentum_out,
    master_out,
    weight_out,
    new_error,
    new_momentum,
    new_master,
    weights,
    grad_in,
    error_in,
    momentum_in,
    master_in,
    merged_high,
    merged_low,
    left_send,
    left_recv,
    left_sum,
    left_all,
    left,
    gram_all,
    vector_rows,
    vector_send,
    vector_all,
    vector_place,
    right_send,
    right_recv,
    right_part,
    right_final,
    right_all,
    basis_in,
    vector_in,
    base_in,
    base_send,
    base_recv,
    ortho_all,
    factor_all,
    right_cat,
    first_sem,
    load_sem,
    rep_send,
    rep_recv,
    grp_send,
    grp_recv,
    strip_sems,
    base_sems,
    ortho_sems,
    x_send,
    x_recv,
    far_core_send,
    far_core_recv,
    plane_send,
    plane_recv,
    core_send,
    core_recv,
):
    me = lax.axis_index("rep")
    my = lax.axis_index("grp")
    columns = grad_query.shape[1]
    gate = grad_gate.shape[1]
    step = 512
    pieces = [(i * step, step, i) for i in range(columns // step)]
    pieces.append((columns, gate, len(pieces)))

    def loads(start, size, index):
        if start < columns:
            grad, error, place = grad_query, error_query, pl.ds(start, size)
        else:
            grad, error, place = grad_gate, error_gate, pl.ds(0, size)
        into = pl.ds(start, size)
        return (
            pltpu.make_async_copy(
                grad.at[:, place], grad_in.at[:, into], load_sem.at[0, index]
            ),
            pltpu.make_async_copy(
                error.at[:, place], error_in.at[:, into], load_sem.at[1, index]
            ),
        )

    side = 4
    y, z, x, core = me // side, me % side, my // 2, my % 2
    place = (y, z)
    block = grad_query.shape[0]
    near = block * 3 // 4
    strip = near // side
    rest = block - near
    wide = (columns + gate) // 2
    cut = -(-wide // 256) * 128

    def wrap(value):
        return lax.rem(value + 2 * side, side)

    def send_base(k, part, source, hop):
        return pltpu.make_async_remote_copy(
            src_ref=source,
            dst_ref=base_recv.at[k, part],
            send_sem=base_sems.at[0, k, part],
            recv_sem=base_sems.at[1, k, part],
            device_id={"grp": wrap(x + hop) * 2 + core},
        )

    def send_ortho(k):
        return pltpu.make_async_remote_copy(
            src_ref=ortho_all.at[0],
            dst_ref=ortho_all.at[k],
            send_sem=ortho_sems.at[0, k],
            recv_sem=ortho_sems.at[1, k],
            device_id={"grp": wrap(x + k) * 2 + core},
        )

    sends = []

    def begin(*copies):
        for copy in copies:
            copy.start()
            sends.append(copy)

    strips = []
    for part in (0, 1):
        those = pl.ds(pl.multiple_of(place[part] * strip, 16), strip)
        low, high = part * wide, (part + 1) * wide
        for i, pair in enumerate(
            ((momentum_query, momentum_gate), (master_query, master_gate))
        ):
            for j, (start, end) in enumerate(
                ((low, min(high, columns)), (max(low, columns), high))
            ):
                if start < end:
                    strips.append(
                        pltpu.make_async_copy(
                            pair[j].at[those, pl.ds(start - j * columns, end - start)],
                            base_in.at[part, i, :, pl.ds(start - low, end - start)],
                            strip_sems.at[part, i, j],
                        )
                    )
    for copy in strips:
        copy.start()

    first = [
        pltpu.make_async_copy(basis_query, basis_in.at[:, pl.ds(0, columns)], first_sem.at[0]),
        pltpu.make_async_copy(basis_gate, basis_in.at[:, pl.ds(columns, gate)], first_sem.at[1]),
        pltpu.make_async_copy(vector_grad, vector_in, first_sem.at[2]),
    ]
    for copy in first:
        copy.start()
    for piece in pieces:
        for copy in loads(*piece):
            copy.start()

    later = [
        pltpu.make_async_copy(source, into.at[:, at], load_sem.at[2 + i, j])
        for i, (into, pair) in enumerate(
            (
                (momentum_in, (momentum_query, momentum_gate)),
                (master_in, (master_query, master_gate)),
            )
        )
        for j, (source, at) in enumerate(zip(pair, (pl.ds(0, columns), pl.ds(columns, gate))))
    ]
    barrier = pltpu.get_barrier_semaphore()

    def greet_rep(d, carry):
        pl.semaphore_signal(barrier, inc=1, device_id={"rep": lax.rem(me + d, reps)})
        return carry

    def greet_grp(d, carry):
        pl.semaphore_signal(barrier, inc=1, device_id={"grp": lax.rem(my + d, grps)})
        return carry

    lax.fori_loop(1, reps, greet_rep, 0)
    lax.fori_loop(1, grps, greet_grp, 0)

    def to_peers(phase, axis, source, target):
        size, index = (reps, me) if axis == "rep" else (grps, my)
        send, recv = (rep_send, rep_recv) if axis == "rep" else (grp_send, grp_recv)

        def copy(d, at):
            peer = lax.rem(index + d, size)
            return pltpu.make_async_remote_copy(
                src_ref=source(peer),
                dst_ref=target.at[at],
                send_sem=send.at[phase, d],
                recv_sem=recv.at[phase, at],
                device_id={axis: peer},
            )

        def start(d, carry):
            copy(d, index).start()
            return carry

        def await_recv(d, carry):
            copy(d, lax.rem(index + d, size)).wait_recv()
            return carry

        def await_send(d, carry):
            copy(d, index).wait_send()
            return carry

        return (
            lambda: lax.fori_loop(1, size, start, 0),
            lambda: lax.fori_loop(1, size, await_recv, 0),
            lambda: lax.fori_loop(1, size, await_send, 0),
        )

    for copy in first:
        copy.wait()
    left_query = jnp.zeros((RANK, grad_query.shape[0]), F32)
    left_gate = left_query
    for start, size, index in pieces:
        if index == 1:
            for copy in strips:
                copy.wait()
            for part in (0, 1):
                base_send[part] = base_in[part, 1] - 0.45 * base_in[part, 0]
            pl.semaphore_wait(barrier, reps - 1 + grps - 1)
            for k, part in ((1, 0), (3, 1), (3, 0), (1, 1)):
                begin(send_base(k, part, base_send.at[part], k))
        for copy in loads(start, size, index):
            copy.wait()
        at = slice(start, start + size)
        high, low = split(grad_in[:, at] + error_in[:, at])
        merged_high[:, at] = high
        merged_low[:, at] = low
        if start < columns:
            basis = split(basis_in[:, at])
            left_query += three_pass(*basis, high, low, NT)
        else:
            basis = split(basis_in[:, at])
            left_gate += three_pass(*basis, high, low, NT)

    for copy in later:
        copy.start()
    length = vector_grad.shape[1]
    lines = -(-length // 128)
    own = jnp.concatenate([left_query, left_gate], axis=0)
    share = BOTH // reps
    left_send[...] = jnp.zeros_like(left_send)
    for i in range(reps):
        left_send[i, 0:share, :] = own[i * share : (i + 1) * share]
    for i in range(lines):
        width = min(128, length - i * 128)
        left_send[i, share : share + 1, 0:width] = vector_in[:, i * 128 : i * 128 + width]

    start_1, recv_1, send_1 = to_peers(0, "rep", lambda peer: left_send.at[peer], left_recv)
    start_1()
    left_recv[me] = left_send[me]
    recv_1()
    total = left_recv[0]
    for i in range(1, reps):
        total += left_recv[i]
    left_sum[...] = total


    start_2, recv_2, send_2 = to_peers(1, "rep", lambda peer: left_sum, left_all)
    start_2()
    left_all[me] = total
    recv_2()
    for i in range(reps):
        left[i * share : (i + 1) * share, :] = left_all[i, 0:share, :]

    left_high, left_low = split(left[...])
    grams = []
    for part in (slice(0, RANK), slice(RANK, BOTH)):
        grams.append(
            three_pass(left_high[part], left_low[part], left_high[part], left_low[part], NT)
        )
    half = RANK // 2
    gram_all[my] = jnp.concatenate(
        [grams[0][:half], grams[0][half:], grams[1][:half], grams[1][half:]], axis=1
    )
    start_3, recv_3, send_3 = to_peers(0, "grp", lambda peer: gram_all.at[my], gram_all)
    start_3()

    vector_rows[...] = jnp.zeros_like(vector_rows)
    for i in range(lines):
        width = min(128, length - i * 128)
        at = slice(i * 128, i * 128 + width)
        mean = left_all[i, share : share + 1, 0:width] / reps
        gain_momentum = 0.9 * vector_momentum[at].reshape(1, width) + mean
        gain = vector_master[at].reshape(1, width) - 0.5 * gain_momentum
        momentum_out[at] = gain_momentum.reshape(width)
        master_out[at] = gain.reshape(width)
        vector_rows[i : i + 1, 0:width] = gain
    vector_send[...] = vector_rows[...].astype(BF16)
    start_v, recv_v, send_v = to_peers(1, "grp", lambda peer: vector_send, vector_all)
    start_v()
    vector_all[my] = vector_send[...]

    recv_3()
    for k, part in ((1, 0), (3, 1)):
        send_base(k, part, base_send.at[part], k).wait_recv()
        begin(send_base(2, part, base_recv.at[k, part], k))
    gram = gram_all[0]
    for i in range(1, grps):
        gram += gram_all[i]
    quarters = [gram[:, i * RANK : (i + 1) * RANK] for i in range(4)]
    query_gram = jnp.concatenate(
        [quarters[0][:, 0:RANK], quarters[1][:, 0:RANK]], axis=0
    )
    gate_gram = jnp.concatenate([quarters[2], quarters[3]], axis=0)
    inverse = inverse_roots(query_gram, gate_gram)
    ortho = full_dot(inverse, left[...])
    ortho_all[0] = ortho
    ortho_high, ortho_low = split(ortho)

    rows = RANK // reps
    for start, size, index in pieces:
        at = slice(start, start + size)
        part = slice(0, RANK) if start < columns else slice(RANK, BOTH)
        terms = three_pass(
            ortho_high[part], ortho_low[part], merged_high[:, at], merged_low[:, at]
        )
        for i in range(reps):
            right_send[i, :, at] = terms[i * rows : (i + 1) * rows]
    start_4, recv_4, send_4 = to_peers(2, "rep", lambda peer: right_send.at[peer], right_recv)
    start_4()
    right_recv[me] = right_send[me]
    begin(*[send_ortho(k) for k in (1, 3, 2)])
    recv_4()
    total = right_recv[0]
    for i in range(1, reps):
        total += right_recv[i]

    right_part[my] = total
    start_5, recv_5, send_5 = to_peers(2, "grp", lambda peer: right_part.at[my], right_part)
    start_5()
    recv_5()
    total = right_part[0]
    for i in range(1, grps):
        total += right_part[i]
    right_final[...] = total

    start_6, recv_6, send_6 = to_peers(3, "rep", lambda peer: right_final, right_all)
    start_6()
    right_all[me] = total

    recv_v()
    low_lanes = lax.broadcasted_iota(jnp.int32, (lines - 1, 128), 1) < 64
    low_lane = lax.broadcasted_iota(jnp.int32, (1, 128), 1) < 64
    for i in range(grps // 2):
        base = i * 2 * length // 128
        even = vector_all[2 * i].astype(F32)
        odd = pltpu.roll(vector_all[2 * i + 1].astype(F32), 64, 1)
        vector_place[base : base + lines - 1, :] = even[: lines - 1]
        vector_place[base + lines - 1 : base + lines, :] = jnp.where(
            low_lane, even[lines - 1 : lines], odd[0:1]
        )
        vector_place[base + lines : base + 2 * lines - 1, :] = jnp.where(
            low_lanes, odd[: lines - 1], odd[1:lines]
        )
    weight_out[...] = vector_place[0 : weight_out.shape[0], :].astype(BF16)

    for k in range(side):
        if k:
            send_ortho(k).wait_recv()
        for i in (0, 1):
            high, low = split(ortho_all[k, i * RANK : (i + 1) * RANK].T / reps)
            factor_all[k, i] = jnp.concatenate([high, high, low], axis=1)
    for k, part in ((3, 0), (1, 1), (2, 0), (2, 1)):
        send_base(k, part, base_send.at[part], 1).wait_recv()

    for copy in later:
        copy.wait()
    recv_6()
    for i in range(reps):
        right_out[i * rows : (i + 1) * rows, :] = right_all[i]
    for start, size, _ in pieces:
        at = slice(start, start + size)
        high, low = split(right_out[:, at])
        right_cat[:, at] = jnp.concatenate([high, low, high], axis=0)

    own_row = my * block

    def finish(first_row, count):
        those = slice(first_row, first_row + count)
        into = pl.ds(pl.multiple_of(own_row + first_row, 16), count)
        for start in range(0, columns + gate, 256):
            at = slice(start, start + 256)
            approx = mm(
                factor_all[0, 0 if start < columns else 1, those, :], right_cat[:, at]
            )
            new_error[those, at] = approx
            old = momentum_in[those, at]
            new_momentum[those, at] = 0.9 * old + approx
            updated = (master_in[those, at] - 0.45 * old) - 0.5 * approx
            new_master[those, at] = updated
            weights[into, at] = updated.astype(BF16)

    def strip_weights(k, part):
        those = pl.ds(pl.multiple_of(place[part] * strip, 16), strip)
        into = pl.ds(pl.multiple_of(rows_of(wrap(x - k), core, place[part]), 16), strip)
        low, high = part * wide, (part + 1) * wide
        bounds = [(low, min(high, columns), 0), (max(low, columns), high, 1)]
        for start, end, which in bounds:
            if start < end:
                approx = mm(factor_all[k, which, those, :], right_cat[:, start:end])
                base = base_recv[k, part, :, start - low : end - low]
                weights[into, start:end] = (base - 0.5 * approx).astype(BF16)

    def move(row, size, start, width, send, recv, **peer):
        span = weights.at[pl.ds(pl.multiple_of(row, 16), size), pl.ds(start, width)]
        return pltpu.make_async_remote_copy(
            src_ref=span, dst_ref=span, send_sem=send, recv_sem=recv, device_id=peer
        )

    def rows_of(from_x, from_core, at):
        return (from_x * 2 + from_core) * block + at * strip

    def columns_of(part, j):
        low = part * wide
        return {2: (low, cut), 0: (low + cut, wide - cut)}.get(j, (low, wide))

    far = ((1, 0, rest), (3, 0, rest), (2, 0, rest // 2), (2, rest // 2, rest // 2))

    def far_span(slot, from_x, from_core):
        _, offset, size = far[slot]
        return rows_of(from_x, from_core, 0) + near + offset, size, 0, columns + gate

    def along_x(slot, from_x, hop):
        return move(
            *far_span(slot, from_x, core),
            x_send.at[slot],
            x_recv.at[slot],
            grp=wrap(x + hop) * 2 + core,
        )

    def far_to_core(slot, from_core):
        return move(
            *far_span(slot, wrap(x - far[slot][0]), from_core),
            far_core_send.at[slot],
            far_core_recv.at[slot],
            grp=x * 2 + 1 - core,
        )

    def in_plane(k, part, j, hop):
        offset = {1: 0, 3: 0, 2: -hop, 0: -hop}[j]
        return strip_move(k, part, j, offset, hop)

    def strip_move(k, part, j, offset, hop):
        peer = (
            wrap(y + hop) * side + z if part == 0 else y * side + wrap(z + hop)
        )
        return move(
            rows_of(wrap(x - k), core, wrap(place[part] + offset)),
            strip,
            *columns_of(part, j),
            plane_send.at[k, part, j],
            plane_recv.at[k, part, j],
            rep=peer,
        )

    landed = {1: -1, 3: 1, 2: -2, 0: -2}

    def to_core(k, part, j, from_core):
        return move(
            rows_of(wrap(x - k), from_core, wrap(place[part] + landed.get(j, 0))),
            strip,
            *columns_of(part, j),
            core_send.at[k, part, j],
            core_recv.at[k, part, j],
            grp=x * 2 + 1 - core,
        )

    def own_to_core(from_core):
        return move(
            rows_of(x, from_core, 0),
            block,
            0,
            columns + gate,
            core_send.at[0, 0, 0],
            core_recv.at[0, 0, 0],
            grp=x * 2 + 1 - core,
        )

    order = [(k, part) for k in (1, 3, 2) for part in (0, 1)]
    for k, part in order:
        if (k, part) == (3, 0):
            finish(near, rest)
            begin(along_x(0, x, 1), along_x(1, x, 3))
        strip_weights(k, part)
        begin(
            in_plane(k, part, 1, 1), in_plane(k, part, 3, 3), to_core(k, part, 4, core)
        )
    finish(0, near)
    begin(own_to_core(core))

    for slot, hop in ((0, 1), (1, 3)):
        along_x(slot, wrap(x - far[slot][0]), hop).wait_recv()
        begin(along_x(slot + 2, wrap(x - far[slot][0]), hop), far_to_core(slot, core))

    def from_neighbours(k, part):
        for j, relayed in ((1, 2), (3, 0)):
            strip_move(k, part, j, landed[j], j).wait_recv()
            begin(in_plane(k, part, relayed, j), to_core(k, part, j, core))

    def from_opposite(k, part):
        for j in (2, 0):
            strip_move(k, part, j, landed[j], 1).wait_recv()
            begin(to_core(k, part, j, core))

    def errors(start):
        at = slice(start, start + 256)
        new_error[:, at] = (grad_in[:, at] + error_in[:, at]) - new_error[:, at]

    tiles = list(range(0, columns + gate, 256))
    for i, (k, part) in enumerate(order):
        from_neighbours(k, part)
        for start in tiles[i :: len(order)]:
            errors(start)
    for k, part in order:
        from_opposite(k, part)
    for slot in (2, 3):
        along_x(slot, wrap(x - 2), 1).wait_recv()
        begin(far_to_core(slot, core))
    own_to_core(1 - core).wait_recv()
    for slot in range(4):
        far_to_core(slot, 1 - core).wait_recv()
    for k, part in order:
        for j in range(5):
            to_core(k, part, j, 1 - core).wait_recv()
    for copy in sends:
        copy.wait_send()
    for wait in (send_1, send_2, send_3, send_v, send_4, send_5, send_6):
        wait()


def write_kernel(columns, *refs):
    right, momentum, master, gains, error, new_momentum, new_master, weights = refs[:8]
    outs, sems = refs[8:-1], refs[-1]
    query, gate = pl.ds(0, columns), pl.ds(columns, right.shape[1] - columns)
    sources = []
    for whole in (weights, error, new_momentum, new_master, right):
        sources += [whole.at[:, query], whole.at[:, gate]]
    copies = [
        pltpu.make_async_copy(source, out, sems.at[i])
        for i, (source, out) in enumerate(zip(sources + [momentum, master, gains], outs))
    ]
    for copy in copies:
        copy.start()
    for copy in copies:
        copy.wait()


def per_device(
    grad_query,
    error_query,
    basis_query,
    momentum_query,
    master_query,
    grad_gate,
    error_gate,
    basis_gate,
    momentum_gate,
    master_gate,
    vector_grad,
    vector_momentum,
    vector_master,
):
    reps, grps = lax.axis_size("rep"), lax.axis_size("grp")
    grad_query, error_query = grad_query[0], error_query[0]
    grad_gate, error_gate = grad_gate[0], error_gate[0]
    rows, columns = grad_query.shape
    gate = grad_gate.shape[1]
    both = columns + gate
    length = vector_grad.shape[1]
    share = RANK // reps
    any_spec = pl.BlockSpec(memory_space=pl.ANY)
    vmem_spec = pl.BlockSpec(memory_space=VMEM)
    held = (
        ((RANK, both), F32),
        ((length,), F32),
        ((length,), F32),
        ((grps * length // 128, 128), BF16),
        ((rows, both), F32),
        ((rows, both), F32),
        ((rows, both), F32),
        ((grps * rows, both), BF16),
    )
    parts = pl.pallas_call(
        functools.partial(factor_kernel, reps, grps),
        out_shape=tuple(VMEM(*entry) for entry in held),
        in_specs=[any_spec] * 7 + [vmem_spec] * 2 + [any_spec] * 4,
        out_specs=[vmem_spec] * len(held),
        scratch_shapes=[
            VMEM((rows, both), F32),
            VMEM((rows, both), F32),
            VMEM((rows, both), F32),
            VMEM((rows, both), F32),
            VMEM((rows, both), BF16),
            VMEM((rows, both), BF16),
            VMEM((reps, 8, rows), F32),
            VMEM((reps, 8, rows), F32),
            VMEM((8, rows), F32),
            VMEM((reps, 8, rows), F32),
            VMEM((BOTH, rows), F32),
            VMEM((grps, RANK // 2, 4 * RANK), F32),
            VMEM((16, 128), F32),
            VMEM((16, 128), BF16),
            VMEM((grps, 16, 128), BF16),
            VMEM((104, 128), F32),
            VMEM((reps, share, both), F32),
            VMEM((reps, share, both), F32),
            VMEM((grps, share, both), F32),
            VMEM((share, both), F32),
            VMEM((reps, share, both), F32),
            VMEM((RANK, both), F32),
            VMEM((1, length), F32),
            VMEM((2, 2, rows * 3 // 16, both // 2), F32),
            VMEM((2, rows * 3 // 16, both // 2), F32),
            VMEM((4, 2, rows * 3 // 16, both // 2), F32),
            VMEM((4, BOTH, rows), F32),
            VMEM((4, 2, rows, 3 * RANK), BF16),
            VMEM((3 * RANK, both), BF16),
            pltpu.SemaphoreType.DMA((3,)),
            pltpu.SemaphoreType.DMA((4, columns // 512 + 1)),
            pltpu.SemaphoreType.DMA((4, reps)),
            pltpu.SemaphoreType.DMA((4, reps)),
            pltpu.SemaphoreType.DMA((3, grps)),
            pltpu.SemaphoreType.DMA((3, grps)),
            pltpu.SemaphoreType.DMA((2, 2, 2)),
            pltpu.SemaphoreType.DMA((2, 4, 2)),
            pltpu.SemaphoreType.DMA((2, 4)),
            pltpu.SemaphoreType.DMA((4,)),
            pltpu.SemaphoreType.DMA((4,)),
            pltpu.SemaphoreType.DMA((4,)),
            pltpu.SemaphoreType.DMA((4,)),
            pltpu.SemaphoreType.DMA((4, 2, 4)),
            pltpu.SemaphoreType.DMA((4, 2, 4)),
            pltpu.SemaphoreType.DMA((4, 2, 5)),
            pltpu.SemaphoreType.DMA((4, 2, 5)),
        ],
        compiler_params=pltpu.CompilerParams(
            collective_id=0, has_side_effects=True, vmem_limit_bytes=40 << 20
        ),
        name="factors",
    )(
        grad_query,
        error_query,
        basis_query.T,
        grad_gate,
        error_gate,
        basis_gate.T,
        vector_grad,
        vector_momentum,
        vector_master,
        momentum_query,
        master_query,
        momentum_gate,
        master_gate,
    )

    def shapes(row_count, dtype):
        return [
            jax.ShapeDtypeStruct((row_count, columns), dtype),
            jax.ShapeDtypeStruct((row_count, gate), dtype),
        ]

    outs = pl.pallas_call(
        functools.partial(write_kernel, columns),
        out_shape=shapes(grps * rows, BF16)
        + shapes(rows, F32) * 3
        + shapes(RANK, F32)
        + [jax.ShapeDtypeStruct(*entry) for entry in held[1:4]],
        in_specs=[vmem_spec] * len(held),
        out_specs=[any_spec] * 13,
        scratch_shapes=[pltpu.SemaphoreType.DMA((13,))],
        compiler_params=pltpu.CompilerParams(vmem_limit_bytes=8 << 20),
        name="write",
    )(*parts)
    return (
        outs[2][None],
        outs[4],
        outs[6],
        outs[0],
        outs[8].T,
        outs[3][None],
        outs[5],
        outs[7],
        outs[1],
        outs[9].T,
        outs[10],
        outs[11],
        outs[12].reshape(grps * length),
    )


def solution(mesh):
    in_specs = (
        P("rep", "grp", None),
        P("rep", "grp", None),
        P(),
        P("grp", None),
        P("grp", None),
        P("rep", "grp", None),
        P("rep", "grp", None),
        P(),
        P("grp", None),
        P("grp", None),
        P("rep", "grp"),
        P("grp"),
        P("grp"),
    )
    out_specs = (
        P("rep", "grp", None),
        P("grp", None),
        P("grp", None),
        P(),
        P(),
        P("rep", "grp", None),
        P("grp", None),
        P("grp", None),
        P(),
        P(),
        P("grp"),
        P("grp"),
        P(),
    )
    return jax.shard_map(
        per_device, mesh=mesh, in_specs=in_specs, out_specs=out_specs, check_vma=False
    )
```
